32 devices in a mesh: grp: 2 (over y), seq: 16 (over z, x, core).
Axes of the slice: x: 2, y: 2, z: 4, core: 2. Of those that a mesh axis runs over, the one named last changes fastest.
Arguments:
- gate_out: bfloat16 [8192, 4096], P(('grp', 'seq')), parts along dimension 0, may hold values from -6 to 6
- gate_in: bfloat16 [8192, 4096], P(('grp', 'seq')), parts along dimension 0, may hold values from -6 to 6
- values: bfloat16 [8192, 4096], P(('grp', 'seq')), parts along dimension 0, may hold values from -6 to 6
- gate_mid: bfloat16 [8192, 4096], P(('grp', 'seq')), parts along dimension 0, may hold values from -6 to 6
- medium_taps: bfloat16 [256, 128], replicated, may hold values from -0.5 to 0.5
- medium_skip: float32 [4096], replicated, may hold values from -3 to 3
- residues: float32 [256, 16], replicated, may hold values from -1 to 1, as said below
- rates: float32 [256, 16], replicated, may hold values from 0 to 0.1, as said below
- long_skip: float32 [4096], replicated, may hold values from -3 to 3
Outputs:
- mixed: bfloat16 [8192, 4096], P(('grp', 'seq')), parts along dimension 0
The draws below stay inside these ranges and needn't reach their ends.
There are 2 independent parts, one for each index of `grp`. The reference program is written for one: setup_inputs(seed, part) draws one part's arguments, and reference() takes and returns one part's arrays. A program takes and returns all parts, laid end to end along the dimension named above; an argument that names none is the same for every part. Nothing has to cross between parts.
Inputs may be any that keep to these rules, and one draw needn't show every extreme that they name: Positive rates; each pole's filter falls by exp(-rate) per position. Real residues of the poles.
All inputs are finite; a program needn't handle non-finite values.
Results may differ from the reference program's by a relative error of at most 0.0061.
Values may be sent and summed in bfloat16 or wider, within the bound.
No kernel may reach another device: no remote copies, remote signals or barrier semaphores. Data moves between devices by JAX's collectives and lax.ppermute only.
A program may use at most 192 MiB of HBM per device.

```python
import jax
import jax.numpy as jnp
from jax import lax

D = 4096
GROUP = 16
GROUPS = 256
MED = 128
POLES = 16
SUB = 128
TOK_DEV = 256
LENGTH = 4096
N_SEQ = 16


def pole_table(key):
    base = jax.random.fold_in(key, 17)
    pick_key, slow_key, fast_key = jax.random.split(base, 3)
    groups = D // GROUP
    slow_share = 0.5
    slow_mask = jax.random.uniform(pick_key, (groups, POLES)) < slow_share
    slow_rate = jnp.exp(jax.random.uniform(slow_key, (groups, POLES), minval=jnp.log(0.05 / LENGTH), maxval=jnp.log(2.3 / LENGTH)))
    fast_rate = jnp.exp(jax.random.uniform(fast_key, (groups, POLES), minval=jnp.log(0.02), maxval=jnp.log(0.1)))
    return jnp.where(slow_mask, slow_rate, fast_rate).astype(jnp.float32)


def draw_rates(key, part):
    return pole_table(key)


def draw_residues(key, part):
    rate_values = pole_table(key)
    noise_key = jax.random.fold_in(key, 29)
    noise_values = jnp.clip(jax.random.normal(noise_key, rate_values.shape), -6.0, 6.0)
    return (noise_values * jnp.sqrt(2.0 * rate_values / POLES)).astype(jnp.float32)


def levels(own_key, extent, cuts, least, high):
    factor_of, own = 1.0, jax.random.fold_in(own_key, 6)
    for position, shards_of in cuts:
        draws = jnp.exp(jax.random.uniform(jax.random.fold_in(own, position), (shards_of,), jnp.float32, least / len(cuts), high / len(cuts)))
        factor_of = factor_of * jnp.repeat(draws, extent[position] // shards_of).reshape([-1 if axis == position else 1 for axis in range(len(extent))])
    return factor_of


def bell_draw(own_key, dims, width, bound, cuts=(), kind=jnp.bfloat16):
    drawn = jax.random.normal(own_key, dims, jnp.float32) * width
    if len(cuts) > 0:
        drawn = levels(own_key, dims, cuts, -0.22, 0.18) * drawn
    return jnp.clip(drawn, min=-bound, max=bound).astype(kind)


def setup_inputs(seed: int = 0, part: int = 0) -> dict:
    splits = jax.random.split(jax.random.key(seed), 10)
    part_splits = jax.random.split(jax.random.fold_in(splits[9], part), 10)
    return {
        "gate_out": bell_draw(part_splits[0], (LENGTH, D), 1.0, 6.0, ((0, 16),)),
        "gate_in": bell_draw(part_splits[1], (LENGTH, D), 1.0, 6.0, ((0, 16),)),
        "values": bell_draw(part_splits[2], (LENGTH, D), 1.0, 6.0, ((0, 16),)),
        "gate_mid": bell_draw(part_splits[3], (LENGTH, D), 1.0, 6.0, ((0, 16),)),
        "medium_taps": bell_draw(splits[4], (GROUPS, MED), MED ** -0.5, 0.5),
        "medium_skip": bell_draw(splits[5], (D,), 0.5, 3.0, (), jnp.float32),
        "residues": draw_residues(jax.random.fold_in(splits[9], 71), part),
        "rates": draw_rates(jax.random.fold_in(splits[9], 71), part),
        "long_skip": bell_draw(splits[8], (D,), 0.5, 3.0, (), jnp.float32),
    }


def banded(tap_values, out_rows, in_cols):
    group_count, tap_count = tap_values.shape
    line = jnp.concatenate([jnp.zeros((group_count, in_cols - tap_count), tap_values.dtype), tap_values[:, ::-1], jnp.zeros((group_count, out_rows - 1), tap_values.dtype)], axis=1)
    cycle = jnp.concatenate([line[:, out_rows - 1:], jnp.zeros((group_count, 1), tap_values.dtype), line[:, :out_rows - 1]], axis=1)
    period = cycle.shape[1]
    tiled = jnp.tile(cycle, (1, out_rows))[:, :out_rows * (period - 1)]
    return tiled.reshape(group_count, out_rows, period - 1)[:, :, :in_cols]


def reference(gate_out, gate_in, values, gate_mid, medium_taps, medium_skip, residues, rates, long_skip):
    block_count = TOK_DEV // SUB
    maximum_level = lax.Precision.HIGHEST
    middle_filter_matrix = banded(medium_taps, SUB, 2 * SUB).astype(jnp.float32)
    offsets = jnp.arange(SUB).astype(jnp.float32)
    decay_up = jnp.exp(-rates[:, :, None] * offsets)
    long_taps = jnp.einsum("gp,gpn->gn", residues, decay_up, precision=maximum_level).astype(jnp.bfloat16)
    short_filter_matrix = banded(long_taps, SUB, SUB).astype(jnp.float32)
    fold_weights = jnp.exp(-rates[:, :, None] * (SUB - 1.0 - offsets)).astype(jnp.bfloat16).astype(jnp.float32)
    distance_weight = residues[:, :, None] * jnp.exp(-rates[:, :, None] * (offsets + 1.0))
    step_decay = jnp.exp(-rates * SUB)[:, :, None]

    def sub_step(held_state, sub_state):
        return step_decay * held_state + sub_state, held_state

    def device_step(carried, pieces):
        rim_rows, held_state = carried
        queries, first_gate, value_rows, middle = pieces
        product = (first_gate.astype(jnp.float32) * value_rows.astype(jnp.float32)).astype(jnp.bfloat16)
        previous = jnp.concatenate([jnp.zeros((SUB - MED + 1, D), jnp.bfloat16), rim_rows, product[:TOK_DEV - SUB]], axis=0)
        sliding_spans = jnp.concatenate([previous.reshape(block_count, SUB, GROUPS, GROUP), product.reshape(block_count, SUB, GROUPS, GROUP)], axis=1)
        medium_conv = jnp.einsum("gts,bsgc->btgc", middle_filter_matrix, sliding_spans.astype(jnp.float32), precision=maximum_level).reshape(TOK_DEV, D)
        medium = medium_conv + medium_skip * product.astype(jnp.float32)
        gated_mid = (middle.astype(jnp.float32) * medium).astype(jnp.bfloat16)
        gate_product_block = gated_mid.reshape(block_count, SUB, GROUPS, GROUP).astype(jnp.float32)
        intra_part = jnp.einsum("gts,bsgc->btgc", short_filter_matrix, gate_product_block, precision=maximum_level)
        sub_states = jnp.einsum("gps,bsgc->bgpc", fold_weights, gate_product_block, precision=maximum_level)
        held_state, preceding_rows = lax.scan(sub_step, held_state, sub_states)
        previous_portion = jnp.einsum("gpt,bgpc->btgc", distance_weight, preceding_rows, precision=maximum_level)
        long_out = (intra_part + previous_portion).reshape(TOK_DEV, D) + long_skip * gated_mid.astype(jnp.float32)
        mixed = (queries.astype(jnp.float32) * long_out).astype(jnp.bfloat16)
        return (product[TOK_DEV - (MED - 1):], held_state), mixed

    start = (jnp.zeros((MED - 1, D), jnp.bfloat16), jnp.zeros((GROUPS, POLES, GROUP), jnp.float32))
    pieces = (gate_out.reshape(N_SEQ, TOK_DEV, D), gate_in.reshape(N_SEQ, TOK_DEV, D),
              values.reshape(N_SEQ, TOK_DEV, D), gate_mid.reshape(N_SEQ, TOK_DEV, D))
    _, mixed = lax.scan(device_step, start, pieces)
    return mixed.reshape(LENGTH, D)
```

```python
import functools

import jax
import jax.numpy as jnp
from jax import lax
from jax.experimental import pallas as pl
from jax.experimental.pallas import tpu as pltpu
from jax.sharding import PartitionSpec as P

MED = 128
SUB = 128
STRIP = 32
LANES = 128
WIDE = 256
BF16 = jnp.bfloat16
F32 = jnp.float32


def dot(a, b, precision=None):
    return jnp.dot(a, b, preferred_element_type=F32, precision=precision)


def own_groups(stack, rows, per_group):
    groups = stack.shape[0] // rows
    owner = lax.broadcasted_iota(jnp.int32, (rows, stack.shape[1]), 1) % LANES // per_group
    kept = stack[:rows]
    for g in range(1, groups):
        kept = jnp.where(owner == g, stack[g * rows : (g + 1) * rows], kept)
    return kept


def toeplitz(line, g):
    spread = jnp.broadcast_to(line[g : g + 1], (STRIP, 2 * LANES))
    return pltpu.roll(spread, 0, 1, stride=1, stride_axis=0)


def pair_of_strips(window, start, depth, lanes):
    return jnp.concatenate(
        [window[start : start + depth, lanes], window[start + STRIP : start + STRIP + depth, lanes]],
        axis=1,
    )


def medium_block(strips, window, lanes, per_group, out):
    for i in range(0, SUB // STRIP, 2):
        spans = pair_of_strips(window, i * STRIP, MED + STRIP, lanes)
        both = own_groups(dot(strips, spans), STRIP, per_group)
        out[i * STRIP : (i + 1) * STRIP, lanes] = both[:, :LANES]
        out[(i + 1) * STRIP : (i + 2) * STRIP, lanes] = both[:, LANES:]


def inner_block(strips, window, lanes, per_group, out):
    for i in range(0, SUB // STRIP, 2):
        spans = pair_of_strips(window, i * STRIP, SUB, lanes)
        both = own_groups(dot(strips, spans), STRIP, per_group)
        out[i * STRIP : (i + 1) * STRIP, lanes] = both[:, :LANES]
        out[(i + 1) * STRIP : (i + 2) * STRIP, lanes] = both[:, LANES:]


def early_kernel(
    per_group, poles,
    gate_in, values, gate_mid, taps, rates, residues, med_skip, long_skip,
    med_strips, long_strips, folds, rates_pc, part, state,
    window, padded, work,
):
    step = pl.program_id(0)
    block = LANES // per_group
    window[...] = (gate_in[...].astype(F32) * values[...].astype(F32)).astype(BF16)
    tap = lax.broadcasted_iota(jnp.int32, (LANES, 2 * LANES), 0)
    spot = lax.broadcasted_iota(jnp.int32, (LANES, 2 * LANES), 1)
    med_line = dot(taps[...], (spot == MED - tap).astype(BF16))
    long_turn = (spot == (SUB - STRIP - tap) % (2 * LANES)).astype(BF16)
    offset = lax.broadcasted_iota(jnp.int32, (LANES, LANES), 1).astype(F32)
    padded[: SUB - STRIP] = jnp.zeros((SUB - STRIP, WIDE), BF16)
    for b in range(WIDE // LANES):
        lanes = slice(b * LANES, (b + 1) * LANES)
        row = step * (WIDE // LANES) + b
        rate_row = rates[pl.ds(row, 1), :]
        residue_row = residues[pl.ds(row, 1), :]
        rate_col = jnp.transpose(jnp.broadcast_to(rate_row, (LANES, LANES)))
        rates_pc[:, lanes] = own_groups(rate_col, poles, per_group)
        decay_up = jnp.exp(-rate_col * offset)
        owner = lax.broadcasted_iota(jnp.int32, (block, LANES), 1) // poles
        mine = lax.broadcasted_iota(jnp.int32, (block, LANES), 0)
        spread = jnp.where(owner == mine, jnp.broadcast_to(residue_row, (block, LANES)), 0.0)
        long_line = dot(
            dot(spread, decay_up, lax.Precision.HIGHEST).astype(BF16), long_turn
        )
        folds[lanes, :] = jnp.exp(-rate_col * (SUB - 1.0 - offset)).astype(BF16)
        for g in range(block):
            rows = slice((b * block + g) * STRIP, (b * block + g + 1) * STRIP)
            med_strips[rows, :] = toeplitz(med_line, b * block + g)[:, : MED + STRIP].astype(BF16)
            long_strips[rows, :] = toeplitz(long_line, g)[:, :LANES].astype(BF16)
        strips = slice(b * block * STRIP, (b + 1) * block * STRIP)
        medium_block(med_strips[strips, :], window, lanes, per_group, work)
        medium = work[:, lanes] + med_skip[:, lanes] * window[SUB:, lanes].astype(F32)
        gated = (gate_mid[:, lanes].astype(F32) * medium).astype(BF16)
        padded[SUB - STRIP :, lanes] = gated
        state[:, lanes] = own_groups(dot(folds[lanes, :], gated), poles, per_group)
        inner_block(long_strips[strips, :], padded, lanes, per_group, part)
        part[:, lanes] = part[:, lanes] + long_skip[:, lanes] * gated.astype(F32)


def late_kernel(
    per_group, poles,
    halo_a, halo_b, gate_in, values, gate_mid, med_strips, folds, rates_pc, med_skip, later,
    gated_out, state, total, message,
    window, work,
):
    block = LANES // per_group
    window[:SUB] = halo_a[...] + halo_b[...]
    window[SUB:] = (gate_in[...].astype(F32) * values[...].astype(F32)).astype(BF16)
    for b in range(WIDE // LANES):
        lanes = slice(b * LANES, (b + 1) * LANES)
        strips = slice(b * block * STRIP, (b + 1) * block * STRIP)
        medium_block(med_strips[strips, :], window, lanes, per_group, work)
        medium = work[:, lanes] + med_skip[:, lanes] * window[SUB:, lanes].astype(F32)
        gated = (gate_mid[:, lanes].astype(F32) * medium).astype(BF16)
        gated_out[:, lanes] = gated
        first = own_groups(dot(folds[lanes, :], gated), poles, per_group)
        state[:, lanes] = first
        whole = jnp.exp(-rates_pc[:, lanes] * SUB) * first + later[:, lanes]
        total[:, lanes] = whole
        message[:, lanes] = whole.astype(BF16)


def inner_kernel(
    per_group, poles,
    gated, long_strips, rates, residues, long_skip,
    part, lift,
    padded,
):
    step = pl.program_id(0)
    block = LANES // per_group
    padded[: SUB - STRIP] = jnp.zeros((SUB - STRIP, WIDE), BF16)
    padded[SUB - STRIP :] = gated[...]
    after = lax.broadcasted_iota(jnp.int32, (SUB, LANES), 0).astype(F32) + 1.0
    for b in range(WIDE // LANES):
        lanes = slice(b * LANES, (b + 1) * LANES)
        row = step * (WIDE // LANES) + b
        lift[:, lanes] = (
            residues[pl.ds(row, 1), :] * jnp.exp(-rates[pl.ds(row, 1), :] * after)
        ).astype(BF16)
        strips = slice(b * block * STRIP, (b + 1) * block * STRIP)
        inner_block(long_strips[strips, :], padded, lanes, per_group, part)
        part[:, lanes] = part[:, lanes] + long_skip[:, lanes] * gated[:, lanes].astype(F32)


def spread_groups(state, per_group, poles):
    tall = jnp.concatenate([state] * (LANES // per_group), axis=0)
    owner = lax.broadcasted_iota(jnp.int32, tall.shape, 1) // per_group
    mine = lax.broadcasted_iota(jnp.int32, tall.shape, 0) // poles
    return jnp.where(owner == mine, tall, 0.0).astype(BF16)


def final_kernel(
    per_group, poles, carry, state, rates_pc, lift, part_a, part_b, gate_out, mixed
):
    for b in range(WIDE // LANES):
        lanes = slice(b * LANES, (b + 1) * LANES)
        start = carry[:, lanes]
        middle = jnp.exp(-rates_pc[:, lanes] * SUB) * start + state[:, lanes]
        before = jnp.concatenate(
            [spread_groups(start, per_group, poles), spread_groups(middle, per_group, poles)],
            axis=1,
        )
        lifted = dot(lift[:, lanes], before)
        for part, rows, own in (
            (part_a, slice(0, SUB), slice(0, LANES)),
            (part_b, slice(SUB, 2 * SUB), slice(LANES, 2 * LANES)),
        ):
            long_out = part[:, lanes] + lifted[:, own]
            mixed[rows, lanes] = (gate_out[rows, lanes].astype(F32) * long_out).astype(BF16)


def cols(rows, first=0):
    return pl.BlockSpec((rows, WIDE), lambda j: (first, j))


def tall(rows, width):
    return pl.BlockSpec((rows, width), lambda j: (j, 0))


def fixed(shape):
    return pl.BlockSpec(shape, lambda j: (0, 0))


def call(kernel, grid, in_specs, outs, scratch, name, flops, args):
    moved = sum(a.size * a.dtype.itemsize for a in args)
    moved += sum(s.size * s.dtype.itemsize for s, _ in outs)
    return pl.pallas_call(
        kernel,
        grid=(grid,),
        in_specs=in_specs,
        out_specs=[spec for _, spec in outs],
        out_shape=[shape for shape, _ in outs],
        scratch_shapes=scratch,
        compiler_params=pltpu.CompilerParams(
            dimension_semantics=("arbitrary",), vmem_limit_bytes=24 << 20
        ),
        cost_estimate=pl.CostEstimate(flops=flops, bytes_accessed=moved, transcendentals=0),
        name=name,
    )(*args)


def swap(value, distance):
    count = lax.axis_size("seq")
    route = [(i, i ^ distance) for i in range(count) if i ^ distance < count]
    return lax.ppermute(value, "seq", route)


def scan_states(total, message, rates_pc, positions):
    count = lax.axis_size("seq")
    index = lax.axis_index("seq")
    upper = index % 2 == 1
    features = total.shape[1]
    half = features // 2
    partner = swap(message, 1).astype(F32)
    decay = jnp.exp(-rates_pc * positions)
    chip = decay * jnp.where(upper, partner, total) + jnp.where(upper, total, partner)
    start = jnp.where(upper, half, 0)
    chip = lax.dynamic_slice_in_dim(chip, start, half, axis=1)
    rates = lax.dynamic_slice_in_dim(rates_pc, start, half, axis=1)
    before = jnp.zeros_like(chip)
    size = 2
    while size < count:
        theirs = swap(chip.astype(BF16), size).astype(F32)
        above = (index // size) % 2 == 1
        behind = (index % size) // 2 * 2 * positions
        before += jnp.where(above, jnp.exp(-rates * behind.astype(F32)) * theirs, 0.0)
        chip = jnp.exp(-rates * (positions * size)) * jnp.where(above, theirs, chip) + jnp.where(
            above, chip, theirs
        )
        size *= 2
    before = before.astype(BF16)
    other = swap(before, 1)
    carry = jnp.concatenate(
        [jnp.where(upper, other, before), jnp.where(upper, before, other)], axis=1
    ).astype(F32)
    return jnp.where(upper, decay * carry + partner, carry)


def shards(
    gate_out, gate_in, values, gate_mid, medium_taps, medium_skip, residues, rates, long_skip
):
    row_count, features = gate_out.shape
    groups, poles = rates.shape
    per_group = features // groups
    count = lax.axis_size("seq")
    steps = features // WIDE
    strip_rows = WIDE // per_group * STRIP
    shape = jax.ShapeDtypeStruct

    tail = (gate_in[row_count - SUB :].astype(F32) * values[row_count - SUB :].astype(F32)).astype(
        BF16
    )
    halo_b = lax.ppermute(tail, "seq", [(i, i + 1) for i in range(1, count - 1, 2)])
    halo_a = lax.ppermute(tail, "seq", [(i, i + 1) for i in range(0, count - 1, 2)])

    rate_rows = rates.reshape(-1, LANES)
    residue_rows = residues.reshape(-1, LANES)
    table = fixed(rate_rows.shape)
    med_skip = medium_skip[None]
    lng_skip = long_skip[None]
    all_strips = groups * STRIP

    med_strips, long_strips, folds, rates_pc, part_b, later = call(
        functools.partial(early_kernel, per_group, poles),
        steps,
        [cols(row_count), cols(row_count), cols(SUB, 1), tall(WIDE // per_group, MED), table, table, cols(1), cols(1)],
        [
            (shape((all_strips, MED + STRIP), BF16), tall(strip_rows, MED + STRIP)),
            (shape((all_strips, SUB), BF16), tall(strip_rows, SUB)),
            (shape((groups * poles, SUB), BF16), tall(WIDE // per_group * poles, SUB)),
            (shape((poles, features), F32), cols(poles)),
            (shape((SUB, features), F32), cols(SUB)),
            (shape((poles, features), F32), cols(poles)),
        ],
        [
            pltpu.VMEM((2 * SUB, WIDE), BF16),
            pltpu.VMEM((2 * SUB - STRIP, WIDE), BF16),
            pltpu.VMEM((SUB, WIDE), F32),
        ],
        "early",
        4 * SUB * SUB * features * 8,
        (gate_in, values, gate_mid, medium_taps, rate_rows, residue_rows, med_skip, lng_skip),
    )
    gated, first, total, message = call(
        functools.partial(late_kernel, per_group, poles),
        steps,
        [cols(SUB), cols(SUB), cols(SUB), cols(SUB), cols(SUB), tall(strip_rows, MED + STRIP),
         tall(WIDE // per_group * poles, SUB), cols(poles), cols(1), cols(poles)],
        [
            (shape((SUB, features), BF16), cols(SUB)),
            (shape((poles, features), F32), cols(poles)),
            (shape((poles, features), F32), cols(poles)),
            (shape((poles, features), BF16), cols(poles)),
        ],
        [pltpu.VMEM((2 * SUB, WIDE), BF16), pltpu.VMEM((SUB, WIDE), F32)],
        "late",
        2 * SUB * SUB * features * 8,
        (halo_a, halo_b, gate_in, values, gate_mid, med_strips, folds, rates_pc, med_skip, later),
    )
    part_a, lift = call(
        functools.partial(inner_kernel, per_group, poles),
        steps,
        [cols(SUB), tall(strip_rows, SUB), table, table, cols(1)],
        [(shape((SUB, features), F32), cols(SUB)), (shape((SUB, features), BF16), cols(SUB))],
        [pltpu.VMEM((2 * SUB - STRIP, WIDE), BF16)],
        "inner",
        2 * SUB * SUB * features * 8,
        (gated, long_strips, rate_rows, residue_rows, lng_skip),
    )
    carry = scan_states(total, message, rates_pc, row_count)
    (mixed,) = call(
        functools.partial(final_kernel, per_group, poles),
        steps,
        [cols(poles), cols(poles), cols(poles), cols(SUB), cols(SUB), cols(SUB), cols(row_count)],
        [(shape((row_count, features), BF16), cols(row_count))],
        [],
        "final",
        2 * SUB * SUB * features * 2,
        (carry, first, rates_pc, lift, part_a, part_b, gate_out),
    )
    return mixed


def solution(mesh):
    rows = P(("grp", "seq"), None)
    return jax.shard_map(
        shards,
        mesh=mesh,
        in_specs=(rows,) * 4 + (P(),) * 5,
        out_specs=rows,
        check_vma=False,
    )
```

```python
import functools

import jax
import jax.numpy as jnp
from jax import lax
from jax.experimental import pallas as pl
from jax.experimental.pallas import tpu as pltpu
from jax.sharding import PartitionSpec as P

MED = 128
SUB = 128
STRIP = 32
LANES = 128
WIDE = 1024
CHUNK = 1024
PIECES = 4
BF16 = jnp.bfloat16
F32 = jnp.float32


def dot(a, b, precision=None):
    return jnp.dot(a, b, preferred_element_type=F32, precision=precision)


def own_groups(stack, rows, per_group):
    groups = stack.shape[0] // rows
    owner = lax.broadcasted_iota(jnp.int32, (rows, stack.shape[1]), 1) % LANES // per_group
    kept = stack[:rows]
    for g in range(1, groups):
        kept = jnp.where(owner == g, stack[g * rows : (g + 1) * rows], kept)
    return kept


def toeplitz(line, g):
    spread = jnp.broadcast_to(line[g : g + 1], (STRIP, 2 * LANES))
    return pltpu.roll(spread, 0, 1, stride=1, stride_axis=0)


def pair_of_strips(window, start, depth, lanes):
    return jnp.concatenate(
        [window[start : start + depth, lanes], window[start + STRIP : start + STRIP + depth, lanes]],
        axis=1,
    )


def medium_block(strips, window, lanes, per_group):
    rows = []
    for i in range(0, SUB // STRIP, 2):
        both = own_groups(
            dot(strips, pair_of_strips(window, i * STRIP, MED + STRIP, lanes)), STRIP, per_group
        )
        rows += [both[:, :LANES], both[:, LANES:]]
    return jnp.concatenate(rows, axis=0)


def inner_block(strips, window, lanes, per_group):
    rows = []
    for i in range(0, SUB // STRIP, 2):
        both = own_groups(
            dot(strips, pair_of_strips(window, i * STRIP, SUB, lanes)), STRIP, per_group
        )
        rows += [both[:, :LANES], both[:, LANES:]]
    return jnp.concatenate(rows, axis=0)


def lanes_at(step, b):
    return pl.ds(pl.multiple_of(step * WIDE + b * LANES, LANES), LANES)


def rows_at(step, b, rows_per_block):
    start = (step * (WIDE // LANES) + b) * rows_per_block
    return pl.ds(pl.multiple_of(start, rows_per_block), rows_per_block)


def early_kernel(
    per_group, poles,
    gate_in, values, gate_mid, taps, rates, med_skip,
    med_strips, folds, rates_pc, product, mid_first, gated_out, state,
    in_buf, value_buf, mid_buf, line, window, sems,
):
    features = gate_in.shape[1]
    block = LANES // per_group
    copies = []
    for c in range(features // CHUNK):
        lanes = pl.ds(c * CHUNK, CHUNK)
        copies.append(
            [
                pltpu.make_async_copy(gate_in.at[:, lanes], in_buf.at[:, lanes], sems.at[c, 0]),
                pltpu.make_async_copy(values.at[:, lanes], value_buf.at[:, lanes], sems.at[c, 1]),
                pltpu.make_async_copy(
                    gate_mid.at[pl.ds(SUB, SUB), lanes], mid_buf.at[:, lanes], sems.at[c, 2]
                ),
                pltpu.make_async_copy(
                    gate_mid.at[pl.ds(0, SUB), lanes], mid_first.at[:, lanes], sems.at[c, 3]
                ),
            ]
        )
        for copy in copies[-1]:
            copy.start()
    tap = lax.broadcasted_iota(jnp.int32, (LANES, 2 * LANES), 0)
    spot = lax.broadcasted_iota(jnp.int32, (LANES, 2 * LANES), 1)
    line[...] = dot(taps[...], (spot == MED - tap).astype(BF16))
    offset = lax.broadcasted_iota(jnp.int32, (LANES, LANES), 1).astype(F32)

    def one(step):
        for b in range(WIDE // LANES):
            at = lanes_at(step, b)
            here = slice(b * LANES, (b + 1) * LANES)
            rate_row = rates[pl.ds(step * (WIDE // LANES) + b, 1), :]
            rate_col = jnp.transpose(jnp.broadcast_to(rate_row, (LANES, LANES)))
            rates_pc[:, at] = own_groups(rate_col, poles, per_group)
            fold = jnp.exp(-rate_col * (SUB - 1.0 - offset)).astype(BF16)
            folds[rows_at(step, b, LANES), :] = fold
            first = (step * (WIDE // LANES) + b) * block
            lines = line[pl.ds(pl.multiple_of(first, block), block), :]
            strips = jnp.concatenate(
                [toeplitz(lines, g)[:, : MED + STRIP].astype(BF16) for g in range(block)], axis=0
            )
            med_strips[rows_at(step, b, block * STRIP), :] = strips
            rows = (in_buf[:, at].astype(F32) * value_buf[:, at].astype(F32)).astype(BF16)
            window[:, here] = rows
            product[:, at] = rows[:SUB]
            medium = medium_block(strips, window, here, per_group)
            medium = medium + med_skip[:, at] * rows[SUB:].astype(F32)
            gated = (mid_buf[:, at].astype(F32) * medium).astype(BF16)
            gated_out[:, at] = gated
            state[:, at] = own_groups(dot(fold, gated), poles, per_group)

    for c in range(features // CHUNK):
        for copy in copies[c]:
            copy.wait()
        pl.loop(c * (CHUNK // WIDE), (c + 1) * (CHUNK // WIDE))(one)


def late_kernel(
    per_group, poles,
    halo, product, gate_mid, med_strips, folds, rates_pc, med_skip, later,
    gated_out, state, total, message,
    window,
):
    features = product.shape[1]
    block = LANES // per_group
    def one(step):
        for b in range(WIDE // LANES):
            at = lanes_at(step, b)
            here = slice(b * LANES, (b + 1) * LANES)
            rows = product[:, at]
            window[:SUB, here] = halo[:, at]
            window[SUB:, here] = rows
            strips = med_strips[rows_at(step, b, block * STRIP), :]
            medium = medium_block(strips, window, here, per_group)
            medium = medium + med_skip[:, at] * rows.astype(F32)
            gated = (gate_mid[:, at].astype(F32) * medium).astype(BF16)
            gated_out[:, at] = gated
            fold = folds[rows_at(step, b, LANES), :]
            first = own_groups(dot(fold, gated), poles, per_group)
            state[:, at] = first
            whole = jnp.exp(-rates_pc[:, at] * SUB) * first + later[:, at]
            total[:, at] = whole
            message[:, at] = whole.astype(BF16)

    pl.loop(0, features // WIDE)(one)


def column(row):
    return jnp.transpose(jnp.broadcast_to(row, (LANES, LANES)))


def inner_kernel(
    per_group, poles, base,
    gated_a, gated_b, rates, residues, long_skip, gate_out,
    part, lift, gate_copy, token,
    taps, line, padded, sem,
):
    width = part.shape[1]
    block = LANES // per_group
    copy = pltpu.make_async_copy(gate_out.at[:, pl.ds(base, width)], gate_copy, sem)
    copy.start()
    offset = lax.broadcasted_iota(jnp.int32, (LANES, LANES), 1).astype(F32)
    after = lax.broadcasted_iota(jnp.int32, (SUB, LANES), 0).astype(F32) + 1.0
    for k in range(2):
        padded[k, : SUB - STRIP] = jnp.zeros((SUB - STRIP, WIDE), BF16)
    for b in range(width // LANES):
        row = slice(base // LANES + b, base // LANES + b + 1)
        rate_row = rates[row, :]
        residue_row = residues[row, :]
        here = slice(b * LANES, (b + 1) * LANES)
        lift[:, here] = (residue_row * jnp.exp(-rate_row * after)).astype(BF16)
        terms = column(residue_row) * jnp.exp(-column(rate_row) * offset)
        taps[b * block : (b + 1) * block, :] = jnp.sum(
            terms.reshape(block, poles, LANES), axis=1
        ).astype(BF16)
    tap = lax.broadcasted_iota(jnp.int32, (LANES, 2 * LANES), 0)
    spot = lax.broadcasted_iota(jnp.int32, (LANES, 2 * LANES), 1)
    turn = (spot == (SUB - STRIP - tap + 2 * LANES) % (2 * LANES)).astype(BF16)
    line[...] = dot(taps[...], turn)

    @pl.loop(0, width // WIDE)
    def _(step):
        for b in range(WIDE // LANES):
            at = lanes_at(step, b)
            source = pl.ds(pl.multiple_of(base + step * WIDE + b * LANES, LANES), LANES)
            here = slice(b * LANES, (b + 1) * LANES)
            lines = line[rows_at(step, b, block), :]
            strips = jnp.concatenate(
                [toeplitz(lines, g)[:, :LANES].astype(BF16) for g in range(block)], axis=0
            )
            for k, gated in enumerate((gated_a, gated_b)):
                rows = gated[:, source]
                padded[k, SUB - STRIP :, here] = rows
                part[k * SUB : (k + 1) * SUB, at] = inner_block(
                    strips, padded.at[k], here, per_group
                ) + long_skip[:, source] * rows.astype(F32)

    token[...] = part[:1, :LANES]
    copy.wait()


def spread_groups(state, per_group, poles):
    tall = jnp.concatenate([state] * (LANES // per_group), axis=0)
    owner = lax.broadcasted_iota(jnp.int32, tall.shape, 1) // per_group
    mine = lax.broadcasted_iota(jnp.int32, tall.shape, 0) // poles
    return jnp.where(owner == mine, tall, 0.0).astype(BF16)


def final_kernel(per_group, poles, own, other, partner, state, rates_pc, *refs):
    parts, lifts, gates = (refs[k * PIECES : (k + 1) * PIECES] for k in range(3))
    mixed, out, sems = refs[3 * PIECES :]
    width = parts[0].shape[1]
    half = own.shape[1]
    positions = mixed.shape[0]
    upper = lax.axis_index("seq") % 2
    copies = []
    for piece, (part, lift, gate) in enumerate(zip(parts, lifts, gates)):

        @pl.loop(0, width // WIDE)
        def _(step):
            for b in range(WIDE // LANES):
                at = lanes_at(step, b)
                to = pl.ds(pl.multiple_of(piece * width + step * WIDE + b * LANES, LANES), LANES)
                side = piece * width // half
                inside = piece * width - side * half + step * WIDE + b * LANES
                inside = pl.ds(pl.multiple_of(inside, LANES), LANES)
                rate = rates_pc[:, to]
                start = jnp.where(upper == side, own[:, inside], other[:, inside].astype(F32))
                device = jnp.exp(-rate * positions) * start + partner[:, to].astype(F32)
                start = jnp.where(upper == 1, device, start)
                middle = jnp.exp(-rate * SUB) * start + state[:, to]
                before = jnp.concatenate(
                    [spread_groups(start, per_group, poles), spread_groups(middle, per_group, poles)],
                    axis=1,
                )
                lifted = dot(lift[:, at], before)
                for k in range(2):
                    rows = slice(k * SUB, (k + 1) * SUB)
                    long_out = part[rows, at] + lifted[:, k * LANES : (k + 1) * LANES]
                    out[rows, to] = (gate[rows, at].astype(F32) * long_out).astype(BF16)

        lanes = pl.ds(piece * width, width)
        copies.append(pltpu.make_async_copy(out.at[:, lanes], mixed.at[:, lanes], sems.at[piece]))
        copies[-1].start()
    for copy in copies:
        copy.wait()


HBM, VMEM, FREE = "hbm", "vmem", "free"


def call(kernel, in_specs, outs, scratch, name, flops, args):
    moved = sum(a.size * a.dtype.itemsize for a in args)
    moved += sum(s.size * s.dtype.itemsize for s, _ in outs)
    spaces = {HBM: pltpu.HBM, VMEM: pltpu.VMEM}
    where = {key: pl.BlockSpec(memory_space=spaces.get(key, pltpu.VMEM)) for key in (HBM, VMEM, FREE)}
    args = [
        pltpu.with_memory_space_constraint(a, spaces[spec]) if spec in spaces else a
        for a, spec in zip(args, in_specs)
    ]
    return pl.pallas_call(
        kernel,
        in_specs=[where[spec] for spec in in_specs],
        out_specs=[where[spec] for _, spec in outs],
        out_shape=[
            pltpu.VMEM(shape.shape, shape.dtype) if spec is VMEM else shape for shape, spec in outs
        ],
        scratch_shapes=scratch,
        compiler_params=pltpu.CompilerParams(vmem_limit_bytes=20 << 20),
        cost_estimate=pl.CostEstimate(flops=flops, bytes_accessed=moved, transcendentals=0),
        name=name,
    )(*args)


def swap(value, distance):
    count = lax.axis_size("seq")
    route = [(i, i ^ distance) for i in range(count) if i ^ distance < count]
    return lax.ppermute(value, "seq", route)


def chip_kernel(positions, total, partner, rates_pc, chip, message, rates):
    half = chip.shape[1]
    upper = lax.axis_index("seq") % 2
    at = pl.ds(pl.multiple_of(upper * half, LANES), half)
    mine, theirs = total[:, at], partner[:, at].astype(F32)
    rate = rates_pc[:, at]
    above = upper == 1
    whole = jnp.exp(-rate * positions) * jnp.where(above, theirs, mine)
    whole += jnp.where(above, mine, theirs)
    chip[...] = whole
    message[...] = whole.astype(BF16)
    rates[...] = rate


def round_kernel(positions, size, last, chip, received, before, rates, chip_out, before_out, message):
    index = lax.axis_index("seq")
    above = (index // size) % 2 == 1
    behind = ((index % size) // 2 * 2 * positions).astype(F32)
    theirs = received[...].astype(F32)
    rate = rates[...]
    mine = chip[...]
    earlier = before[...] + jnp.where(above, jnp.exp(-rate * behind) * theirs, 0.0)
    before_out[...] = earlier
    whole = jnp.exp(-rate * (positions * size)) * jnp.where(above, theirs, mine)
    whole += jnp.where(above, mine, theirs)
    chip_out[...] = whole
    message[...] = (earlier if last else whole).astype(BF16)


def scan_states(total, message, rates_pc, positions, fill):
    count = lax.axis_size("seq")
    poles, features = total.shape
    half = jax.ShapeDtypeStruct((poles, features // 2), F32)
    packed = jax.ShapeDtypeStruct((poles, features // 2), BF16)
    partner = swap(fill(message), 1)
    chip, message, rates = call(
        functools.partial(chip_kernel, positions), [VMEM] * 3,
        [(half, VMEM), (packed, VMEM), (half, VMEM)], [], "chip", total.size, (total, partner, rates_pc),
    )
    before = jnp.zeros_like(chip)
    if count == 2:
        message = jnp.zeros_like(message)
    size = 2
    while size < count:
        received = swap(fill(message), size)
        chip, before, message = call(
            functools.partial(round_kernel, positions, size, 2 * size >= count),
            [VMEM, VMEM, FREE if size == 2 else VMEM, VMEM],
            [(half, VMEM), (half, VMEM), (packed, VMEM)],
            [], "round", total.size, (chip, received, before, rates),
        )
        size *= 2
    return before, swap(fill(message), 1), partner


def shards(
    gate_out, gate_in, values, gate_mid, medium_taps, medium_skip, residues, rates, long_skip
):
    row_count, features = gate_out.shape
    groups, poles = rates.shape
    per_group = features // groups
    count = lax.axis_size("seq")
    width = features // PIECES
    shape = jax.ShapeDtypeStruct
    dma = pltpu.SemaphoreType.DMA
    chunks = features // CHUNK

    tail = (gate_in[row_count - SUB :].astype(F32) * values[row_count - SUB :].astype(F32)).astype(
        BF16
    )
    halo = lax.ppermute(tail, "seq", [(i, i + 1) for i in range(count - 1)])

    rate_rows = rates.reshape(-1, LANES)
    residue_rows = residues.reshape(-1, LANES)
    med_skip = medium_skip[None]
    lng_skip = long_skip[None]
    per_pole = shape((poles, features), F32)
    half_rows = shape((SUB, features), BF16)

    med_strips, folds, rates_pc, product, mid_first, gated_b, later = call(
        functools.partial(early_kernel, per_group, poles),
        [HBM, HBM, HBM, FREE, FREE, FREE],
        [
            (shape((groups * STRIP, MED + STRIP), BF16), VMEM),
            (shape((groups * poles, SUB), BF16), VMEM),
            (per_pole, VMEM),
            (half_rows, VMEM),
            (half_rows, VMEM),
            (half_rows, VMEM),
            (per_pole, VMEM),
        ],
        [
            pltpu.VMEM((row_count, features), BF16),
            pltpu.VMEM((row_count, features), BF16),
            pltpu.VMEM((SUB, features), BF16),
            pltpu.VMEM((groups, 2 * LANES), F32),
            pltpu.VMEM((2 * SUB, WIDE), BF16),
            dma((chunks, 4)),
        ],
        "early",
        2 * SUB * SUB * features * 8,
        (gate_in, values, gate_mid, medium_taps, rate_rows, med_skip),
    )
    gated_a, first, total, message = call(
        functools.partial(late_kernel, per_group, poles),
        [VMEM] * 6 + [FREE, VMEM],
        [(half_rows, VMEM), (per_pole, VMEM), (per_pole, VMEM), (shape((poles, features), BF16), VMEM)],
        [pltpu.VMEM((2 * SUB, WIDE), BF16)],
        "late",
        2 * SUB * SUB * features * 8,
        (halo, product, mid_first, med_strips, folds, rates_pc, med_skip, later),
    )

    def inner(piece, rate_rows):
        return call(
            functools.partial(inner_kernel, per_group, poles, piece * width),
            [VMEM, VMEM, FREE, FREE, FREE, HBM],
            [
                (shape((row_count, width), F32), VMEM),
                (shape((SUB, width), BF16), VMEM),
                (shape((row_count, width), BF16), VMEM),
                (shape((1, LANES), F32), VMEM),
            ],
            [
                pltpu.VMEM((width // per_group, LANES), BF16),
                pltpu.VMEM((width // per_group, 2 * LANES), F32),
                pltpu.VMEM((2, 2 * SUB - STRIP, WIDE), BF16),
                dma,
            ],
            f"inner{piece}",
            4 * SUB * SUB * width * 8,
            (gated_a, gated_b, rate_rows, residue_rows, lng_skip, gate_out),
        )

    pieces = []

    def fill(message):
        if len(pieces) < PIECES:
            tokens = [piece[-1] for piece in pieces]
            message, held, _ = lax.optimization_barrier((message, rate_rows, tokens))
            pieces.append(inner(len(pieces), held))
        else:
            message, _ = lax.optimization_barrier((message, pieces[-1][-1]))
        return message

    before, other, partner = scan_states(total, message, rates_pc, row_count, fill)
    while len(pieces) < PIECES:
        fill(message)
    parts, lifts, gates, _ = zip(*pieces)
    (mixed,) = call(
        functools.partial(final_kernel, per_group, poles),
        [VMEM] * (5 + 3 * PIECES),
        [(shape((row_count, features), BF16), HBM)],
        [pltpu.VMEM((row_count, features), BF16), dma((PIECES,))],
        "final",
        2 * SUB * SUB * features * 2,
        (before, other, partner, first, rates_pc, *parts, *lifts, *gates),
    )
    return mixed


def solution(mesh):
    rows = P(("grp", "seq"), None)
    return jax.shard_map(
        shards,
        mesh=mesh,
        in_specs=(rows,) * 4 + (P(),) * 5,
        out_specs=rows,
        check_vma=False,
    )
```

```python
import functools

import jax
import jax.numpy as jnp
from jax import lax
from jax.experimental import pallas as pl
from jax.experimental.pallas import tpu as pltpu
from jax.sharding import PartitionSpec as P

MED = 128
SUB = 128
STRIP = 32
LANES = 128
WIDE = 1024
CHUNK = 1024
PIECES = 3
BF16 = jnp.bfloat16
F32 = jnp.float32


def dot(a, b, precision=None):
    return jnp.dot(a, b, preferred_element_type=F32, precision=precision)


def own_groups(stack, rows, per_group):
    groups = stack.shape[0] // rows
    owner = lax.broadcasted_iota(jnp.int32, (rows, stack.shape[1]), 1) % LANES // per_group
    kept = stack[:rows]
    for g in range(1, groups):
        kept = jnp.where(owner == g, stack[g * rows : (g + 1) * rows], kept)
    return kept


def toeplitz(line, g):
    spread = jnp.broadcast_to(line[g : g + 1], (STRIP, 2 * LANES))
    return pltpu.roll(spread, 0, 1, stride=1, stride_axis=0)


def filter_block(strips, window, depth, per_group):
    rows = []
    for i in range(0, SUB // STRIP, 2):
        first, second = i * STRIP, (i + 1) * STRIP
        spans = jnp.concatenate([window[first : first + depth], window[second : second + depth]], axis=1)
        both = own_groups(dot(strips, spans), STRIP, per_group)
        rows += [both[:, :LANES], both[:, LANES:]]
    return jnp.concatenate(rows, axis=0)


def lanes_at(step, b):
    return pl.ds(pl.multiple_of(step * WIDE + b * LANES, LANES), LANES)


def rows_at(step, b, rows_per_block):
    start = (step * (WIDE // LANES) + b) * rows_per_block
    return pl.ds(pl.multiple_of(start, rows_per_block), rows_per_block)


def tail_kernel(gate_in, values, product, held, sems):
    last, features = gate_in.shape[0] - SUB, gate_in.shape[1]
    copies = []
    for c in range(features // CHUNK):
        lanes = pl.ds(c * CHUNK, CHUNK)
        for k, source in enumerate((gate_in, values)):
            copy = pltpu.make_async_copy(
                source.at[pl.ds(last, SUB), lanes], held.at[k, :, lanes], sems.at[c, k]
            )
            copy.start()
            copies.append(copy)
    for c in range(features // CHUNK):
        copies[2 * c].wait()
        copies[2 * c + 1].wait()
        lanes = slice(c * CHUNK, (c + 1) * CHUNK)
        product[:, lanes] = (held[0, :, lanes].astype(F32) * held[1, :, lanes].astype(F32)).astype(
            BF16
        )


def early_kernel(
    per_group, poles,
    gate_in, values, gate_mid, taps, rates, med_skip,
    med_strips, folds, rates_pc, product, mid_first, gated_out, state,
    in_buf, value_buf, mid_buf, line, sems,
):
    features = gate_in.shape[1]
    block = LANES // per_group
    copies = []
    for c in range(features // CHUNK):
        lanes = pl.ds(c * CHUNK, CHUNK)
        copies.append(
            [
                pltpu.make_async_copy(gate_in.at[:, lanes], in_buf.at[:, lanes], sems.at[c, 0]),
                pltpu.make_async_copy(values.at[:, lanes], value_buf.at[:, lanes], sems.at[c, 1]),
                pltpu.make_async_copy(
                    gate_mid.at[pl.ds(SUB, SUB), lanes], mid_buf.at[:, lanes], sems.at[c, 2]
                ),
                pltpu.make_async_copy(
                    gate_mid.at[pl.ds(0, SUB), lanes], mid_first.at[:, lanes], sems.at[c, 3]
                ),
            ]
        )
        for copy in copies[-1]:
            copy.start()
    tap = lax.broadcasted_iota(jnp.int32, (LANES, 2 * LANES), 0)
    spot = lax.broadcasted_iota(jnp.int32, (LANES, 2 * LANES), 1)
    line[...] = dot(taps[...], (spot == MED - tap).astype(BF16))
    offset = lax.broadcasted_iota(jnp.int32, (LANES, LANES), 1).astype(F32)

    def one(step):
        for b in range(WIDE // LANES):
            at = lanes_at(step, b)
            rate_row = rates[pl.ds(step * (WIDE // LANES) + b, 1), :]
            rate_col = jnp.transpose(jnp.broadcast_to(rate_row, (LANES, LANES)))
            rates_pc[:, at] = own_groups(rate_col, poles, per_group)
            fold = jnp.exp(-rate_col * (SUB - 1.0 - offset)).astype(BF16)
            folds[rows_at(step, b, LANES), :] = fold
            first = (step * (WIDE // LANES) + b) * block
            lines = line[pl.ds(pl.multiple_of(first, block), block), :]
            strips = jnp.concatenate(
                [toeplitz(lines, g)[:, : MED + STRIP].astype(BF16) for g in range(block)], axis=0
            )
            med_strips[rows_at(step, b, block * STRIP), :] = strips
            rows = (in_buf[:, at].astype(F32) * value_buf[:, at].astype(F32)).astype(BF16)
            product[:, at] = rows[:SUB]
            medium = filter_block(strips, rows, MED + STRIP, per_group)
            medium = medium + med_skip[:, at] * rows[SUB:].astype(F32)
            gated = (mid_buf[:, at].astype(F32) * medium).astype(BF16)
            gated_out[:, at] = gated
            state[:, at] = own_groups(dot(fold, gated), poles, per_group)

    for c in range(features // CHUNK):
        for copy in copies[c]:
            copy.wait()
        pl.loop(c * (CHUNK // WIDE), (c + 1) * (CHUNK // WIDE))(one)


def late_kernel(
    per_group, poles, followed,
    halo, product, gate_mid, med_strips, folds, rates_pc, med_skip, later,
    gated_out, state, total, message,
):
    half = total.shape[1]
    block = LANES // per_group
    side = lax.axis_index("seq") % 2
    side = side if followed else 1 - side

    base = pl.multiple_of(side * half, half)
    for b in range(half // LANES):
        at = pl.ds(pl.multiple_of(base + b * LANES, LANES), LANES)
        to = slice(b * LANES, (b + 1) * LANES)
        tall = block * STRIP
        spot = pl.multiple_of(side * (half // LANES * tall), tall) + b * tall
        rows = product[:, at]
        window = jnp.concatenate([halo[:, at], rows], axis=0)
        strips = med_strips[pl.ds(pl.multiple_of(spot, tall), tall), :]
        medium = filter_block(strips, window, MED + STRIP, per_group)
        medium = medium + med_skip[:, at] * rows.astype(F32)
        gated = (gate_mid[:, at].astype(F32) * medium).astype(BF16)
        gated_out[:, to] = gated
        first = own_groups(dot(folds[at, :], gated), poles, per_group)
        state[:, to] = first
        whole = jnp.exp(-rates_pc[:, at] * SUB) * first + later[:, at]
        total[:, to] = whole
        message[:, to] = whole.astype(BF16)


def column(row):
    return jnp.transpose(jnp.broadcast_to(row, (LANES, LANES)))


def inner_kernel(
    per_group, poles, base,
    other_a, own_a, gated_b, rates, residues, long_skip, gate_out,
    part, lift, gate_copy, token,
    taps, line, gated_a, sem,
):
    width = part.shape[1]
    half = own_a.shape[1]
    upper = lax.axis_index("seq") % 2
    block = LANES // per_group
    for core in range(2):

        @pl.when(upper == core)
        def _():
            for b in range(width // LANES):
                side, inside = divmod(base + b * LANES, half)
                source = own_a if side == core else other_a
                gated_a[:, b * LANES : (b + 1) * LANES] = source[:, inside : inside + LANES]

    copy = pltpu.make_async_copy(gate_out.at[:, pl.ds(base, width)], gate_copy, sem)
    copy.start()
    offset = lax.broadcasted_iota(jnp.int32, (LANES, LANES), 1).astype(F32)
    after = lax.broadcasted_iota(jnp.int32, (SUB, LANES), 0).astype(F32) + 1.0
    for b in range(width // LANES):
        row = slice(base // LANES + b, base // LANES + b + 1)
        rate_row = rates[row, :]
        residue_row = residues[row, :]
        here = slice(b * LANES, (b + 1) * LANES)
        lift[:, here] = (residue_row * jnp.exp(-rate_row * after)).astype(BF16)
        terms = column(residue_row) * jnp.exp(-column(rate_row) * offset)
        taps[b * block : (b + 1) * block, :] = jnp.sum(
            terms.reshape(block, poles, LANES), axis=1
        ).astype(BF16)
    tap = lax.broadcasted_iota(jnp.int32, (LANES, 2 * LANES), 0)
    spot = lax.broadcasted_iota(jnp.int32, (LANES, 2 * LANES), 1)
    turn = (spot == (SUB - STRIP - tap + 2 * LANES) % (2 * LANES)).astype(BF16)
    line[...] = dot(taps[...], turn)

    for b in range(width // LANES):
        at = slice(b * LANES, (b + 1) * LANES)
        source = slice(base + b * LANES, base + (b + 1) * LANES)
        lines = line[b * block : (b + 1) * block, :]
        strips = jnp.concatenate(
            [toeplitz(lines, g)[:, :LANES].astype(BF16) for g in range(block)], axis=0
        )
        for k, rows in enumerate((gated_a[:, at], gated_b[:, source])):
            window = jnp.concatenate([jnp.zeros((SUB - STRIP, LANES), BF16), rows], axis=0)
            part[k * SUB : (k + 1) * SUB, at] = filter_block(
                strips, window, SUB, per_group
            ) + long_skip[:, source] * rows.astype(F32)

    token[...] = part[:1, :LANES]
    copy.wait()


def spread_groups(state, per_group, poles):
    tall = jnp.concatenate([state] * (LANES // per_group), axis=0)
    owner = lax.broadcasted_iota(jnp.int32, tall.shape, 1) // per_group
    mine = lax.broadcasted_iota(jnp.int32, tall.shape, 0) // poles
    return jnp.where(owner == mine, tall, 0.0).astype(BF16)


def final_kernel(per_group, poles, own, other, own_state, other_state, rates_pc, *refs):
    parts, lifts, gates = (refs[k * PIECES : (k + 1) * PIECES] for k in range(3))
    mixed, out, sems = refs[3 * PIECES :]
    half = own.shape[1]
    upper = lax.axis_index("seq") % 2
    copies = []
    base = 0
    for piece, (part, lift, gate) in enumerate(zip(parts, lifts, gates)):
        width = part.shape[1]
        for b in range(width // LANES):
            at = slice(b * LANES, (b + 1) * LANES)
            to = slice(base + b * LANES, base + (b + 1) * LANES)
            side, inside = divmod(base + b * LANES, half)
            inside = slice(inside, inside + LANES)
            mine = upper == side
            start = jnp.where(mine, own[:, inside], other[:, inside].astype(F32))
            state = jnp.where(mine, own_state[:, inside], other_state[:, inside])
            middle = jnp.exp(-rates_pc[:, to] * SUB) * start + state
            before = jnp.concatenate(
                [spread_groups(start, per_group, poles), spread_groups(middle, per_group, poles)],
                axis=1,
            )
            lifted = dot(lift[:, at], before)
            for k in range(2):
                rows = slice(k * SUB, (k + 1) * SUB)
                long_out = part[rows, at] + lifted[:, k * LANES : (k + 1) * LANES]
                out[rows, to] = (gate[rows, at].astype(F32) * long_out).astype(BF16)
        lanes = pl.ds(base, width)
        copies.append(pltpu.make_async_copy(out.at[:, lanes], mixed.at[:, lanes], sems.at[piece]))
        copies[-1].start()
        base += width
    for copy in copies:
        copy.wait()


HBM, VMEM, FREE = "hbm", "vmem", "free"


def call(kernel, in_specs, outs, scratch, name, flops, args):
    moved = sum(a.size * a.dtype.itemsize for a in args)
    moved += sum(s.size * s.dtype.itemsize for s, _ in outs)
    spaces = {HBM: pltpu.HBM, VMEM: pltpu.VMEM}
    where = {key: pl.BlockSpec(memory_space=spaces.get(key, pltpu.VMEM)) for key in (HBM, VMEM, FREE)}
    args = [
        pltpu.with_memory_space_constraint(a, spaces[spec]) if spec in spaces else a
        for a, spec in zip(args, in_specs)
    ]
    return pl.pallas_call(
        kernel,
        in_specs=[where[spec] for spec in in_specs],
        out_specs=[where[spec] for _, spec in outs],
        out_shape=[
            pltpu.VMEM(shape.shape, shape.dtype) if spec is VMEM else shape for shape, spec in outs
        ],
        scratch_shapes=scratch,
        compiler_params=pltpu.CompilerParams(vmem_limit_bytes=20 << 20),
        cost_estimate=pl.CostEstimate(flops=flops, bytes_accessed=moved, transcendentals=0),
        name=name,
    )(*args)


def swap(value, distance):
    count = lax.axis_size("seq")
    route = [(i, i ^ distance) for i in range(count) if i ^ distance < count]
    return lax.ppermute(value, "seq", route)


def chip_kernel(positions, total, partner, rates_pc, chip, before, message, rates):
    half = chip.shape[1]
    upper = lax.axis_index("seq") % 2
    above = upper == 1
    mine, theirs = total[...], partner[...].astype(F32)
    rate = rates_pc[:, pl.ds(pl.multiple_of(upper * half, LANES), half)]
    whole = jnp.exp(-rate * positions) * jnp.where(above, theirs, mine)
    whole += jnp.where(above, mine, theirs)
    chip[...] = whole
    before[...] = jnp.zeros_like(whole)
    message[...] = whole.astype(BF16)
    rates[...] = rate


def grown(positions, size, chip, received, before, rates):
    index = lax.axis_index("seq")
    above = (index // size) % 2 == 1
    behind = ((index % size) // 2 * 2 * positions).astype(F32)
    rate, mine, theirs = rates[...], chip[...], received[...].astype(F32)
    earlier = before[...] + jnp.where(above, jnp.exp(-rate * behind) * theirs, 0.0)
    whole = jnp.exp(-rate * (positions * size)) * jnp.where(above, theirs, mine)
    return earlier, whole + jnp.where(above, mine, theirs)


def round_kernel(
    positions, size, chip, received, before, rates, _, chip_out, before_out, message
):
    before_out[...], whole = grown(positions, size, chip, received, before, rates)
    chip_out[...] = whole
    message[...] = whole.astype(BF16)


def last_kernel(
    positions, size, chip, received, before, rates, total, partner, _, carry, message
):
    upper = lax.axis_index("seq") % 2 == 1
    earlier, _ = grown(positions, size, chip, received, before, rates)
    lower = jnp.where(upper, partner[...].astype(F32), total[...])
    after = jnp.exp(-rates[...] * positions) * earlier + lower
    carry[...] = jnp.where(upper, after, earlier)
    message[...] = jnp.where(upper, earlier, after).astype(BF16)


def scan_states(total, partner, rates_pc, positions, fill):
    count = lax.axis_size("seq")
    half = jax.ShapeDtypeStruct(total.shape, F32)
    packed = jax.ShapeDtypeStruct(total.shape, BF16)
    chip, before, message, rates = call(
        functools.partial(chip_kernel, positions), [VMEM] * 3,
        [(half, VMEM), (half, VMEM), (packed, VMEM), (half, VMEM)],
        [], "chip", total.size, (total, partner, rates_pc),
    )
    size = 2
    while True:
        message, filled = fill(message)
        received = swap(message, size)
        held = (chip, received, before, rates)
        if 2 * size >= count:
            break
        chip, before, message = call(
            functools.partial(round_kernel, positions, size), [VMEM] * 5,
            [(half, VMEM), (half, VMEM), (packed, VMEM)],
            [], "round", total.size, (*held, filled),
        )
        size *= 2
    carry, message = call(
        functools.partial(last_kernel, positions, size), [VMEM] * 7,
        [(half, VMEM), (packed, VMEM)],
        [], "last", total.size, (*held, total, partner, filled),
    )
    message, _ = fill(message)
    return carry, swap(message, 1)


def shards(
    gate_out, gate_in, values, gate_mid, medium_taps, medium_skip, residues, rates, long_skip
):
    row_count, features = gate_out.shape
    groups, poles = rates.shape
    per_group = features // groups
    count = lax.axis_size("seq")
    cuts = [features // LANES * k // PIECES * LANES for k in range(PIECES + 1)]
    shape = jax.ShapeDtypeStruct
    dma = pltpu.SemaphoreType.DMA
    chunks = features // CHUNK

    (tail,) = call(
        tail_kernel,
        [HBM, HBM],
        [(shape((SUB, features), BF16), VMEM)],
        [pltpu.VMEM((2, SUB, features), BF16), dma((chunks, 2))],
        "tail",
        SUB * features,
        (gate_in, values),
    )
    halo = lax.ppermute(tail, "seq", [(i, i + 1) for i in range(count - 1)])

    rate_rows = rates.reshape(-1, LANES)
    residue_rows = residues.reshape(-1, LANES)
    med_skip = medium_skip[None]
    lng_skip = long_skip[None]
    rate_rows, residue_rows, med_skip, lng_skip = lax.optimization_barrier(
        (rate_rows, residue_rows, med_skip, lng_skip)
    )
    per_pole = shape((poles, features), F32)
    half_rows = shape((SUB, features), BF16)

    med_strips, folds, rates_pc, product, mid_first, gated_b, later = call(
        functools.partial(early_kernel, per_group, poles),
        [HBM, HBM, HBM, FREE, FREE, FREE],
        [
            (shape((groups * STRIP, MED + STRIP), BF16), VMEM),
            (shape((groups * poles, SUB), BF16), VMEM),
            (per_pole, VMEM),
            (half_rows, VMEM),
            (half_rows, VMEM),
            (half_rows, VMEM),
            (per_pole, VMEM),
        ],
        [
            pltpu.VMEM((row_count, features), BF16),
            pltpu.VMEM((row_count, features), BF16),
            pltpu.VMEM((SUB, features), BF16),
            pltpu.VMEM((groups, 2 * LANES), F32),
            dma((chunks, 4)),
        ],
        "early",
        2 * SUB * SUB * features * 8,
        (gate_in, values, gate_mid, medium_taps, rate_rows, med_skip),
    )
    half_states = shape((poles, features // 2), F32)

    def late(followed, med_skip):
        return call(
            functools.partial(late_kernel, per_group, poles, followed),
            [VMEM] * 6 + [FREE, VMEM],
            [
                (shape((SUB, features // 2), BF16), VMEM),
                (half_states, VMEM),
                (half_states, VMEM),
                (shape((poles, features // 2), BF16), VMEM),
            ],
            [],
            "late",
            SUB * SUB * features * 8,
            (halo, product, mid_first, med_strips, folds, rates_pc, med_skip, later),
        )

    other_a, other_state, _, message = late(False, med_skip)
    message, held = lax.optimization_barrier((message, med_skip))
    partner = swap(message, 1)
    own_a, own_state, total, _ = late(True, held)

    def inner(piece, residue_rows):
        width = cuts[piece + 1] - cuts[piece]
        return call(
            functools.partial(inner_kernel, per_group, poles, cuts[piece]),
            [VMEM, VMEM, VMEM, FREE, FREE, FREE, HBM],
            [
                (shape((row_count, width), F32), VMEM),
                (shape((SUB, width), BF16), VMEM),
                (shape((row_count, width), BF16), VMEM),
                (shape((1, LANES), F32), VMEM),
            ],
            [
                pltpu.VMEM((width // per_group, LANES), BF16),
                pltpu.VMEM((width // per_group, 2 * LANES), F32),
                pltpu.VMEM((SUB, width), BF16),
                dma,
            ],
            f"inner{piece}",
            4 * SUB * SUB * width * 8,
            (other_a, own_a, gated_b, rate_rows, residue_rows, lng_skip, gate_out),
        )

    pieces = []

    def fill(message):
        if len(pieces) < PIECES:
            message, held = lax.optimization_barrier((message, residue_rows))
            pieces.append(inner(len(pieces), held))
        return message, pieces[-1][-1]

    carry, other = scan_states(total, partner, rates_pc, row_count, fill)
    while len(pieces) < PIECES:
        fill(other)
    parts, lifts, gates, _ = zip(*pieces)
    (mixed,) = call(
        functools.partial(final_kernel, per_group, poles),
        [VMEM] * (5 + 3 * PIECES),
        [(shape((row_count, features), BF16), HBM)],
        [pltpu.VMEM((row_count, features), BF16), dma((PIECES,))],
        "final",
        2 * SUB * SUB * features * 2,
        (carry, other, own_state, other_state, rates_pc, *parts, *lifts, *gates),
    )
    return mixed


def solution(mesh):
    rows = P(("grp", "seq"), None)
    return jax.shard_map(
        shards,
        mesh=mesh,
        in_specs=(rows,) * 4 + (P(),) * 5,
        out_specs=rows,
        check_vma=False,
    )
```

```python
import functools

import jax
import jax.numpy as jnp
from jax import lax
from jax.experimental import pallas as pl
from jax.experimental.pallas import tpu as pltpu
from jax.sharding import PartitionSpec as P

MED = 128
SUB = 128
STRIP = 32
LANES = 128
WIDE = 1024
CHUNK = 1024
PIECES = 3
BF16 = jnp.bfloat16
F32 = jnp.float32


def dot(a, b, precision=None):
    return jnp.dot(a, b, preferred_element_type=F32, precision=precision)


def own_groups(stack, rows, per_group):
    groups = stack.shape[0] // rows
    owner = lax.broadcasted_iota(jnp.int32, (rows, stack.shape[1]), 1) % LANES // per_group
    kept = stack[:rows]
    for g in range(1, groups):
        kept = jnp.where(owner == g, stack[g * rows : (g + 1) * rows], kept)
    return kept


def toeplitz(line, g):
    spread = jnp.broadcast_to(line[g : g + 1], (STRIP, 2 * LANES))
    return pltpu.roll(spread, 0, 1, stride=1, stride_axis=0)


def filter_block(strips, window, depth, per_group):
    rows = []
    for i in range(0, SUB // STRIP, 2):
        first, second = i * STRIP, (i + 1) * STRIP
        spans = jnp.concatenate([window[first : first + depth], window[second : second + depth]], axis=1)
        both = own_groups(dot(strips, spans), STRIP, per_group)
        rows += [both[:, :LANES], both[:, LANES:]]
    return jnp.concatenate(rows, axis=0)


def lanes_at(step, b):
    return pl.ds(pl.multiple_of(step * WIDE + b * LANES, LANES), LANES)


def rows_at(step, b, rows_per_block):
    start = (step * (WIDE // LANES) + b) * rows_per_block
    return pl.ds(pl.multiple_of(start, rows_per_block), rows_per_block)


def tail_kernel(gate_in, values, product, held, sems):
    last, features = gate_in.shape[0] - SUB, gate_in.shape[1]
    copies = []
    for c in range(features // CHUNK):
        lanes = pl.ds(c * CHUNK, CHUNK)
        for k, source in enumerate((gate_in, values)):
            copy = pltpu.make_async_copy(
                source.at[pl.ds(last, SUB), lanes], held.at[k, :, lanes], sems.at[c, k]
            )
            copy.start()
            copies.append(copy)
    for c in range(features // CHUNK):
        copies[2 * c].wait()
        copies[2 * c + 1].wait()
        lanes = slice(c * CHUNK, (c + 1) * CHUNK)
        product[:, lanes] = (held[0, :, lanes].astype(F32) * held[1, :, lanes].astype(F32)).astype(
            BF16
        )


def early_kernel(
    per_group, poles,
    gate_in, values, gate_mid, taps, rates, med_skip,
    med_strips, folds, rates_pc, product, mid_first, gated_out, state,
    in_buf, value_buf, mid_buf, line, sems,
):
    features = gate_in.shape[1]
    block = LANES // per_group
    copies = []
    for c in range(features // CHUNK):
        lanes = pl.ds(c * CHUNK, CHUNK)
        copies.append(
            [
                pltpu.make_async_copy(gate_in.at[:, lanes], in_buf.at[:, lanes], sems.at[c, 0]),
                pltpu.make_async_copy(values.at[:, lanes], value_buf.at[:, lanes], sems.at[c, 1]),
                pltpu.make_async_copy(
                    gate_mid.at[pl.ds(SUB, SUB), lanes], mid_buf.at[:, lanes], sems.at[c, 2]
                ),
                pltpu.make_async_copy(
                    gate_mid.at[pl.ds(0, SUB), lanes], mid_first.at[:, lanes], sems.at[c, 3]
                ),
            ]
        )
        for copy in copies[-1]:
            copy.start()
    tap = lax.broadcasted_iota(jnp.int32, (LANES, 2 * LANES), 0)
    spot = lax.broadcasted_iota(jnp.int32, (LANES, 2 * LANES), 1)
    line[...] = dot(taps[...], (spot == MED - tap).astype(BF16))
    offset = lax.broadcasted_iota(jnp.int32, (LANES, LANES), 1).astype(F32)

    def one(step):
        for b in range(WIDE // LANES):
            at = lanes_at(step, b)
            rate_row = rates[pl.ds(step * (WIDE // LANES) + b, 1), :]
            rate_col = jnp.transpose(jnp.broadcast_to(rate_row, (LANES, LANES)))
            rates_pc[:, at] = own_groups(rate_col, poles, per_group)
            fold = jnp.exp(-rate_col * (SUB - 1.0 - offset)).astype(BF16)
            folds[rows_at(step, b, LANES), :] = fold
            first = (step * (WIDE // LANES) + b) * block
            lines = line[pl.ds(pl.multiple_of(first, block), block), :]
            strips = jnp.concatenate(
                [toeplitz(lines, g)[:, : MED + STRIP].astype(BF16) for g in range(block)], axis=0
            )
            med_strips[rows_at(step, b, block * STRIP), :] = strips
            rows = (in_buf[:, at].astype(F32) * value_buf[:, at].astype(F32)).astype(BF16)
            product[:, at] = rows[:SUB]
            medium = filter_block(strips, rows, MED + STRIP, per_group)
            medium = medium + med_skip[:, at] * rows[SUB:].astype(F32)
            gated = (mid_buf[:, at].astype(F32) * medium).astype(BF16)
            gated_out[:, at] = gated
            state[:, at] = own_groups(dot(fold, gated), poles, per_group)

    for c in range(features // CHUNK):
        for copy in copies[c]:
            copy.wait()
        pl.loop(c * (CHUNK // WIDE), (c + 1) * (CHUNK // WIDE))(one)


def late_kernel(
    per_group, poles, followed,
    halo, product, gate_mid, med_strips, folds, rates_pc, med_skip, later,
    gated_out, state, total, message,
):
    half = total.shape[1]
    block = LANES // per_group
    side = lax.axis_index("seq") % 2
    side = side if followed else 1 - side

    base = pl.multiple_of(side * half, half)
    for b in range(half // LANES):
        at = pl.ds(pl.multiple_of(base + b * LANES, LANES), LANES)
        to = slice(b * LANES, (b + 1) * LANES)
        tall = block * STRIP
        spot = pl.multiple_of(side * (half // LANES * tall), tall) + b * tall
        rows = product[:, at]
        window = jnp.concatenate([halo[:, at], rows], axis=0)
        strips = med_strips[pl.ds(pl.multiple_of(spot, tall), tall), :]
        medium = filter_block(strips, window, MED + STRIP, per_group)
        medium = medium + med_skip[:, at] * rows.astype(F32)
        gated = (gate_mid[:, at].astype(F32) * medium).astype(BF16)
        gated_out[:, to] = gated
        first = own_groups(dot(folds[at, :], gated), poles, per_group)
        state[:, to] = first
        whole = jnp.exp(-rates_pc[:, at] * SUB) * first + later[:, at]
        total[:, to] = whole
        message[:, to] = whole.astype(BF16)


def column(row):
    return jnp.transpose(jnp.broadcast_to(row, (LANES, LANES)))


def inner_kernel(
    per_group, poles, base,
    other_a, own_a, gated_b, rates, residues, long_skip, gate_out,
    part, lift, gate_copy, token,
    taps, line, gated_a, sem,
):
    width = part.shape[1]
    half = own_a.shape[1]
    upper = lax.axis_index("seq") % 2
    block = LANES // per_group
    for core in range(2):

        @pl.when(upper == core)
        def _():
            for b in range(width // LANES):
                side, inside = divmod(base + b * LANES, half)
                source = own_a if side == core else other_a
                gated_a[:, b * LANES : (b + 1) * LANES] = source[:, inside : inside + LANES]

    copy = pltpu.make_async_copy(gate_out.at[:, pl.ds(base, width)], gate_copy, sem)
    copy.start()
    offset = lax.broadcasted_iota(jnp.int32, (LANES, LANES), 1).astype(F32)
    after = lax.broadcasted_iota(jnp.int32, (SUB, LANES), 0).astype(F32) + 1.0
    for b in range(width // LANES):
        row = slice(base // LANES + b, base // LANES + b + 1)
        rate_row = rates[row, :]
        residue_row = residues[row, :]
        here = slice(b * LANES, (b + 1) * LANES)
        lift[:, here] = (residue_row * jnp.exp(-rate_row * after)).astype(BF16)
        terms = column(residue_row) * jnp.exp(-column(rate_row) * offset)
        taps[b * block : (b + 1) * block, :] = jnp.sum(
            terms.reshape(block, poles, LANES), axis=1
        ).astype(BF16)
    tap = lax.broadcasted_iota(jnp.int32, (LANES, 2 * LANES), 0)
    spot = lax.broadcasted_iota(jnp.int32, (LANES, 2 * LANES), 1)
    turn = (spot == (SUB - STRIP - tap + 2 * LANES) % (2 * LANES)).astype(BF16)
    line[...] = dot(taps[...], turn)

    for b in range(width // LANES):
        at = slice(b * LANES, (b + 1) * LANES)
        source = slice(base + b * LANES, base + (b + 1) * LANES)
        lines = line[b * block : (b + 1) * block, :]
        strips = jnp.concatenate(
            [toeplitz(lines, g)[:, :LANES].astype(BF16) for g in range(block)], axis=0
        )
        for k, rows in enumerate((gated_a[:, at], gated_b[:, source])):
            window = jnp.concatenate([jnp.zeros((SUB - STRIP, LANES), BF16), rows], axis=0)
            part[k * SUB : (k + 1) * SUB, at] = filter_block(
                strips, window, SUB, per_group
            ) + long_skip[:, source] * rows.astype(F32)

    token[...] = part[:1, :LANES]
    copy.wait()


def spread_groups(state, per_group, poles):
    tall = jnp.concatenate([state] * (LANES // per_group), axis=0)
    owner = lax.broadcasted_iota(jnp.int32, tall.shape, 1) // per_group
    mine = lax.broadcasted_iota(jnp.int32, tall.shape, 0) // poles
    return jnp.where(owner == mine, tall, 0.0).astype(BF16)


def final_kernel(per_group, poles, followed, carry, state, rates_pc, *refs):
    parts, lifts, gates = (refs[k * PIECES : (k + 1) * PIECES] for k in range(3))
    mixed, out, sems = refs[-3:]
    half = carry.shape[1]
    upper = lax.axis_index("seq") % 2
    places = [
        (piece, b * LANES)
        for piece, part in enumerate(parts)
        for b in range(part.shape[1] // LANES)
    ]

    def write(side):
        copies = []
        for n in range(half // LANES):
            piece, base = places[side * (half // LANES) + n]
            at = slice(base, base + LANES)
            here = slice(n * LANES, (n + 1) * LANES)
            to = slice(side * half + n * LANES, side * half + (n + 1) * LANES)
            start = carry[:, here].astype(F32)
            middle = jnp.exp(-rates_pc[:, to] * SUB) * start + state[:, here]
            before = jnp.concatenate(
                [spread_groups(start, per_group, poles), spread_groups(middle, per_group, poles)],
                axis=1,
            )
            lifted = dot(lifts[piece][:, at], before)
            for k in range(2):
                rows = slice(k * SUB, (k + 1) * SUB)
                long_out = parts[piece][rows, at] + lifted[:, k * LANES : (k + 1) * LANES]
                out[rows, here] = (gates[piece][rows, at].astype(F32) * long_out).astype(BF16)
            if (n + 1) * LANES % CHUNK == 0:
                first = (n + 1) * LANES - CHUNK
                copy = pltpu.make_async_copy(
                    out.at[:, pl.ds(first, CHUNK)],
                    mixed.at[:, pl.ds(side * half + first, CHUNK)],
                    sems.at[first // CHUNK],
                )
                copy.start()
                copies.append(copy)
        for copy in copies:
            copy.wait()

    for core in range(2):
        pl.when(upper == core)(functools.partial(write, core if followed else 1 - core))


HBM, VMEM, FREE = "hbm", "vmem", "free"


def call(kernel, in_specs, outs, scratch, name, flops, args, aliases={}):
    moved = sum(a.size * a.dtype.itemsize for a in args)
    moved += sum(s.size * s.dtype.itemsize for s, _ in outs)
    spaces = {HBM: pltpu.HBM, VMEM: pltpu.VMEM}
    where = {key: pl.BlockSpec(memory_space=spaces.get(key, pltpu.VMEM)) for key in (HBM, VMEM, FREE)}
    args = [
        pltpu.with_memory_space_constraint(a, spaces[spec]) if spec in spaces else a
        for a, spec in zip(args, in_specs)
    ]
    return pl.pallas_call(
        kernel,
        in_specs=[where[spec] for spec in in_specs],
        out_specs=[where[spec] for _, spec in outs],
        out_shape=[
            pltpu.VMEM(shape.shape, shape.dtype) if spec is VMEM else shape for shape, spec in outs
        ],
        scratch_shapes=scratch,
        input_output_aliases=aliases,
        compiler_params=pltpu.CompilerParams(vmem_limit_bytes=20 << 20),
        cost_estimate=pl.CostEstimate(flops=flops, bytes_accessed=moved, transcendentals=0),
        name=name,
    )(*args)


def swap(value, distance):
    count = lax.axis_size("seq")
    route = [(i, i ^ distance) for i in range(count) if i ^ distance < count]
    return lax.ppermute(value, "seq", route)


def chip_kernel(positions, total, partner, rates_pc, chip, before, message, rates):
    half = chip.shape[1]
    upper = lax.axis_index("seq") % 2
    above = upper == 1
    mine, theirs = total[...], partner[...].astype(F32)
    rate = rates_pc[:, pl.ds(pl.multiple_of(upper * half, LANES), half)]
    whole = jnp.exp(-rate * positions) * jnp.where(above, theirs, mine)
    whole += jnp.where(above, mine, theirs)
    chip[...] = whole
    before[...] = jnp.zeros_like(whole)
    message[...] = whole.astype(BF16)
    rates[...] = rate


def grown(positions, size, chip, received, before, rates):
    index = lax.axis_index("seq")
    above = (index // size) % 2 == 1
    behind = ((index % size) // 2 * 2 * positions).astype(F32)
    rate, mine, theirs = rates[...], chip[...], received[...].astype(F32)
    earlier = before[...] + jnp.where(above, jnp.exp(-rate * behind) * theirs, 0.0)
    whole = jnp.exp(-rate * (positions * size)) * jnp.where(above, theirs, mine)
    return earlier, whole + jnp.where(above, mine, theirs)


def round_kernel(
    positions, size, chip, received, before, rates, _, chip_out, before_out, message
):
    before_out[...], whole = grown(positions, size, chip, received, before, rates)
    chip_out[...] = whole
    message[...] = whole.astype(BF16)


def last_kernel(
    positions, size, chip, received, before, rates, total, partner, _, carry, message
):
    upper = lax.axis_index("seq") % 2 == 1
    earlier, _ = grown(positions, size, chip, received, before, rates)
    lower = jnp.where(upper, partner[...].astype(F32), total[...])
    after = jnp.exp(-rates[...] * positions) * earlier + lower
    carry[...] = jnp.where(upper, after, earlier)
    message[...] = jnp.where(upper, earlier, after).astype(BF16)


def scan_states(total, partner, rates_pc, positions, fill):
    count = lax.axis_size("seq")
    half = jax.ShapeDtypeStruct(total.shape, F32)
    packed = jax.ShapeDtypeStruct(total.shape, BF16)
    chip, before, message, rates = call(
        functools.partial(chip_kernel, positions), [VMEM] * 3,
        [(half, VMEM), (half, VMEM), (packed, VMEM), (half, VMEM)],
        [], "chip", total.size, (total, partner, rates_pc),
    )
    size = 2
    while True:
        message, filled = fill(message)
        received = swap(message, size)
        held = (chip, received, before, rates)
        if 2 * size >= count:
            break
        chip, before, message = call(
            functools.partial(round_kernel, positions, size), [VMEM] * 5,
            [(half, VMEM), (half, VMEM), (packed, VMEM)],
            [], "round", total.size, (*held, filled),
        )
        size *= 2
    carry, message = call(
        functools.partial(last_kernel, positions, size), [VMEM] * 7,
        [(half, VMEM), (packed, VMEM)],
        [], "last", total.size, (*held, total, partner, filled),
    )
    message, _ = fill(message)
    return carry, swap(message, 1)


def shards(
    gate_out, gate_in, values, gate_mid, medium_taps, medium_skip, residues, rates, long_skip
):
    row_count, features = gate_out.shape
    groups, poles = rates.shape
    per_group = features // groups
    count = lax.axis_size("seq")
    cuts = [features // LANES * k // PIECES * LANES for k in range(PIECES + 1)]
    shape = jax.ShapeDtypeStruct
    dma = pltpu.SemaphoreType.DMA
    chunks = features // CHUNK

    (tail,) = call(
        tail_kernel,
        [HBM, HBM],
        [(shape((SUB, features), BF16), VMEM)],
        [pltpu.VMEM((2, SUB, features), BF16), dma((chunks, 2))],
        "tail",
        SUB * features,
        (gate_in, values),
    )
    halo = lax.ppermute(tail, "seq", [(i, i + 1) for i in range(count - 1)])

    rate_rows = rates.reshape(-1, LANES)
    residue_rows = residues.reshape(-1, LANES)
    med_skip = medium_skip[None]
    lng_skip = long_skip[None]
    rate_rows, residue_rows, med_skip, lng_skip = lax.optimization_barrier(
        (rate_rows, residue_rows, med_skip, lng_skip)
    )
    per_pole = shape((poles, features), F32)
    half_rows = shape((SUB, features), BF16)

    med_strips, folds, rates_pc, product, mid_first, gated_b, later = call(
        functools.partial(early_kernel, per_group, poles),
        [HBM, HBM, HBM, FREE, FREE, FREE],
        [
            (shape((groups * STRIP, MED + STRIP), BF16), VMEM),
            (shape((groups * poles, SUB), BF16), VMEM),
            (per_pole, VMEM),
            (half_rows, VMEM),
            (half_rows, VMEM),
            (half_rows, VMEM),
            (per_pole, VMEM),
        ],
        [
            pltpu.VMEM((row_count, features), BF16),
            pltpu.VMEM((row_count, features), BF16),
            pltpu.VMEM((SUB, features), BF16),
            pltpu.VMEM((groups, 2 * LANES), F32),
            dma((chunks, 4)),
        ],
        "early",
        2 * SUB * SUB * features * 8,
        (gate_in, values, gate_mid, medium_taps, rate_rows, med_skip),
    )
    half_states = shape((poles, features // 2), F32)

    def late(followed, med_skip):
        return call(
            functools.partial(late_kernel, per_group, poles, followed),
            [VMEM] * 6 + [FREE, VMEM],
            [
                (shape((SUB, features // 2), BF16), VMEM),
                (half_states, VMEM),
                (half_states, VMEM),
                (shape((poles, features // 2), BF16), VMEM),
            ],
            [],
            "late",
            SUB * SUB * features * 8,
            (halo, product, mid_first, med_strips, folds, rates_pc, med_skip, later),
        )

    other_a, other_state, _, message = late(False, med_skip)
    message, held = lax.optimization_barrier((message, med_skip))
    partner = swap(message, 1)
    own_a, own_state, total, _ = late(True, held)

    def inner(piece, residue_rows):
        width = cuts[piece + 1] - cuts[piece]
        return call(
            functools.partial(inner_kernel, per_group, poles, cuts[piece]),
            [VMEM, VMEM, VMEM, FREE, FREE, FREE, HBM],
            [
                (shape((row_count, width), F32), VMEM),
                (shape((SUB, width), BF16), VMEM),
                (shape((row_count, width), BF16), VMEM),
                (shape((1, LANES), F32), VMEM),
            ],
            [
                pltpu.VMEM((width // per_group, LANES), BF16),
                pltpu.VMEM((width // per_group, 2 * LANES), F32),
                pltpu.VMEM((SUB, width), BF16),
                dma,
            ],
            f"inner{piece}",
            4 * SUB * SUB * width * 8,
            (other_a, own_a, gated_b, rate_rows, residue_rows, lng_skip, gate_out),
        )

    pieces = []

    def fill(message):
        if len(pieces) < PIECES:
            message, held = lax.optimization_barrier((message, residue_rows))
            pieces.append(inner(len(pieces), held))
        return message, pieces[-1][-1]

    carry, other = scan_states(total, partner, rates_pc, row_count, fill)
    while len(pieces) < PIECES:
        fill(other)
    parts, lifts, gates, _ = zip(*pieces)

    def final(followed, carry, state, *earlier):
        (mixed,) = call(
            functools.partial(final_kernel, per_group, poles, followed),
            [VMEM] * (3 + 3 * PIECES) + [HBM] * len(earlier),
            [(shape((row_count, features), BF16), HBM)],
            [pltpu.VMEM((row_count, features // 2), BF16), dma((chunks // 2,))],
            "final",
            SUB * SUB * features * 2,
            (carry, state, rates_pc, *parts, *lifts, *gates, *earlier),
            {3 + 3 * PIECES: 0} if earlier else {},
        )
        return mixed

    mixed = final(True, carry, own_state)
    return final(False, other, other_state, mixed)


def solution(mesh):
    rows = P(("grp", "seq"), None)
    return jax.shard_map(
        shards,
        mesh=mesh,
        in_specs=(rows,) * 4 + (P(),) * 5,
        out_specs=rows,
        check_vma=False,
    )
```

```python
import functools

import jax
import jax.numpy as jnp
from jax import lax
from jax.experimental import pallas as pl
from jax.experimental.pallas import tpu as pltpu
from jax.sharding import PartitionSpec as P

MED = 128
SUB = 128
STRIP = 32
LANES = 128
WIDE = 1024
CHUNK = 1024
PIECES = 3
BF16 = jnp.bfloat16
F32 = jnp.float32


def dot(a, b, precision=None):
    return jnp.dot(a, b, preferred_element_type=F32, precision=precision)


def own_groups(stack, rows, per_group):
    groups = stack.shape[0] // rows
    owner = lax.broadcasted_iota(jnp.int32, (rows, stack.shape[1]), 1) % LANES // per_group
    kept = stack[:rows]
    for g in range(1, groups):
        kept = jnp.where(owner == g, stack[g * rows : (g + 1) * rows], kept)
    return kept


def toeplitz(line, g):
    spread = jnp.broadcast_to(line[g : g + 1], (STRIP, 2 * LANES))
    return pltpu.roll(spread, 0, 1, stride=1, stride_axis=0)


def filter_block(strips, window, depth, per_group):
    rows = []
    for i in range(0, SUB // STRIP, 2):
        first, second = i * STRIP, (i + 1) * STRIP
        spans = jnp.concatenate([window[first : first + depth], window[second : second + depth]], axis=1)
        both = own_groups(dot(strips, spans), STRIP, per_group)
        rows += [both[:, :LANES], both[:, LANES:]]
    return jnp.concatenate(rows, axis=0)


def lanes_at(step, b):
    return pl.ds(pl.multiple_of(step * WIDE + b * LANES, LANES), LANES)


def rows_at(step, b, rows_per_block):
    start = (step * (WIDE // LANES) + b) * rows_per_block
    return pl.ds(pl.multiple_of(start, rows_per_block), rows_per_block)


def tail_kernel(gate_in, values, product, held, sems):
    last, features = gate_in.shape[0] - SUB, gate_in.shape[1]
    copies = []
    for c in range(features // CHUNK):
        lanes = pl.ds(c * CHUNK, CHUNK)
        for k, source in enumerate((gate_in, values)):
            copy = pltpu.make_async_copy(
                source.at[pl.ds(last, SUB), lanes], held.at[k, :, lanes], sems.at[c, k]
            )
            copy.start()
            copies.append(copy)
    for c in range(features // CHUNK):
        copies[2 * c].wait()
        copies[2 * c + 1].wait()
        lanes = slice(c * CHUNK, (c + 1) * CHUNK)
        product[:, lanes] = (held[0, :, lanes].astype(F32) * held[1, :, lanes].astype(F32)).astype(
            BF16
        )


def early_kernel(
    per_group, poles,
    gate_in, values, gate_mid, taps, rates, med_skip,
    med_strips, folds, rates_pc, product, mid_first, gated_out, state,
    in_buf, value_buf, mid_buf, line, sems,
):
    features = gate_in.shape[1]
    block = LANES // per_group
    copies = []
    for c in range(features // CHUNK):
        lanes = pl.ds(c * CHUNK, CHUNK)
        copies.append(
            [
                pltpu.make_async_copy(gate_in.at[:, lanes], in_buf.at[:, lanes], sems.at[c, 0]),
                pltpu.make_async_copy(values.at[:, lanes], value_buf.at[:, lanes], sems.at[c, 1]),
                pltpu.make_async_copy(
                    gate_mid.at[pl.ds(SUB, SUB), lanes], mid_buf.at[:, lanes], sems.at[c, 2]
                ),
                pltpu.make_async_copy(
                    gate_mid.at[pl.ds(0, SUB), lanes], mid_first.at[:, lanes], sems.at[c, 3]
                ),
            ]
        )
        for copy in copies[-1]:
            copy.start()
    tap = lax.broadcasted_iota(jnp.int32, (LANES, 2 * LANES), 0)
    spot = lax.broadcasted_iota(jnp.int32, (LANES, 2 * LANES), 1)
    line[...] = dot(taps[...], (spot == MED - tap).astype(BF16))
    offset = lax.broadcasted_iota(jnp.int32, (LANES, LANES), 1).astype(F32)

    def one(step):
        for b in range(WIDE // LANES):
            at = lanes_at(step, b)
            rate_row = rates[pl.ds(step * (WIDE // LANES) + b, 1), :]
            rate_col = jnp.transpose(jnp.broadcast_to(rate_row, (LANES, LANES)))
            rates_pc[:, at] = own_groups(rate_col, poles, per_group)
            fold = jnp.exp(-rate_col * (SUB - 1.0 - offset)).astype(BF16)
            folds[rows_at(step, b, LANES), :] = fold
            first = (step * (WIDE // LANES) + b) * block
            lines = line[pl.ds(pl.multiple_of(first, block), block), :]
            strips = jnp.concatenate(
                [toeplitz(lines, g)[:, : MED + STRIP].astype(BF16) for g in range(block)], axis=0
            )
            med_strips[rows_at(step, b, block * STRIP), :] = strips
            rows = (in_buf[:, at].astype(F32) * value_buf[:, at].astype(F32)).astype(BF16)
            product[:, at] = rows[:SUB]
            medium = filter_block(strips, rows, MED + STRIP, per_group)
            medium = medium + med_skip[:, at] * rows[SUB:].astype(F32)
            gated = (mid_buf[:, at].astype(F32) * medium).astype(BF16)
            gated_out[:, at] = gated
            state[:, at] = own_groups(dot(fold, gated), poles, per_group)

    for c in range(features // CHUNK):
        for copy in copies[c]:
            copy.wait()
        pl.loop(c * (CHUNK // WIDE), (c + 1) * (CHUNK // WIDE))(one)


def late_kernel(
    per_group, poles, followed,
    halo, product, gate_mid, med_strips, folds, rates_pc, med_skip, later,
    gated_out, state, total, message,
):
    half = total.shape[1]
    block = LANES // per_group
    side = lax.axis_index("seq") % 2
    side = side if followed else 1 - side

    base = pl.multiple_of(side * half, half)
    for b in range(half // LANES):
        at = pl.ds(pl.multiple_of(base + b * LANES, LANES), LANES)
        to = slice(b * LANES, (b + 1) * LANES)
        tall = block * STRIP
        spot = pl.multiple_of(side * (half // LANES * tall), tall) + b * tall
        rows = product[:, at]
        window = jnp.concatenate([halo[:, at], rows], axis=0)
        strips = med_strips[pl.ds(pl.multiple_of(spot, tall), tall), :]
        medium = filter_block(strips, window, MED + STRIP, per_group)
        medium = medium + med_skip[:, at] * rows.astype(F32)
        gated = (gate_mid[:, at].astype(F32) * medium).astype(BF16)
        gated_out[:, to] = gated
        first = own_groups(dot(folds[at, :], gated), poles, per_group)
        state[:, to] = first
        whole = jnp.exp(-rates_pc[:, at] * SUB) * first + later[:, at]
        total[:, to] = whole
        message[:, to] = whole.astype(BF16)


def column(row):
    return jnp.transpose(jnp.broadcast_to(row, (LANES, LANES)))


def inner_kernel(
    per_group, poles, base,
    other_a, own_a, gated_b, rates, residues, long_skip, gate_out,
    part, lift, gate_copy, token,
    taps, line, gated_a, sem,
):
    width = part.shape[1]
    half = own_a.shape[1]
    upper = lax.axis_index("seq") % 2
    block = LANES // per_group
    for core in range(2):

        @pl.when(upper == core)
        def _():
            for b in range(width // LANES):
                side, inside = divmod(base + b * LANES, half)
                source = own_a if side == core else other_a
                gated_a[:, b * LANES : (b + 1) * LANES] = source[:, inside : inside + LANES]

    copy = pltpu.make_async_copy(gate_out.at[:, pl.ds(base, width)], gate_copy, sem)
    copy.start()
    offset = lax.broadcasted_iota(jnp.int32, (LANES, LANES), 1).astype(F32)
    after = lax.broadcasted_iota(jnp.int32, (SUB, LANES), 0).astype(F32) + 1.0
    for b in range(width // LANES):
        row = slice(base // LANES + b, base // LANES + b + 1)
        rate_row = rates[row, :]
        residue_row = residues[row, :]
        here = slice(b * LANES, (b + 1) * LANES)
        lift[:, here] = (residue_row * jnp.exp(-rate_row * after)).astype(BF16)
        terms = column(residue_row) * jnp.exp(-column(rate_row) * offset)
        taps[b * block : (b + 1) * block, :] = jnp.sum(
            terms.reshape(block, poles, LANES), axis=1
        ).astype(BF16)
    tap = lax.broadcasted_iota(jnp.int32, (LANES, 2 * LANES), 0)
    spot = lax.broadcasted_iota(jnp.int32, (LANES, 2 * LANES), 1)
    turn = (spot == (SUB - STRIP - tap + 2 * LANES) % (2 * LANES)).astype(BF16)
    line[...] = dot(taps[...], turn)

    for b in range(width // LANES):
        at = slice(b * LANES, (b + 1) * LANES)
        source = slice(base + b * LANES, base + (b + 1) * LANES)
        lines = line[b * block : (b + 1) * block, :]
        strips = jnp.concatenate(
            [toeplitz(lines, g)[:, :LANES].astype(BF16) for g in range(block)], axis=0
        )
        for k, rows in enumerate((gated_a[:, at], gated_b[:, source])):
            window = jnp.concatenate([jnp.zeros((SUB - STRIP, LANES), BF16), rows], axis=0)
            part[k * SUB : (k + 1) * SUB, at] = filter_block(
                strips, window, SUB, per_group
            ) + long_skip[:, source] * rows.astype(F32)

    token[...] = part[:1, :LANES]
    copy.wait()


def spread_groups(state, per_group, poles):
    tall = jnp.concatenate([state] * (LANES // per_group), axis=0)
    owner = lax.broadcasted_iota(jnp.int32, tall.shape, 1) // per_group
    mine = lax.broadcasted_iota(jnp.int32, tall.shape, 0) // poles
    return jnp.where(owner == mine, tall, 0.0).astype(BF16)


def final_kernel(per_group, poles, followed, carry, state, rates_pc, *refs):
    parts, lifts, gates = (refs[k * PIECES : (k + 1) * PIECES] for k in range(3))
    mixed, out, sems = refs[-3:]
    half = carry.shape[1]
    upper = lax.axis_index("seq") % 2
    places = [
        (piece, b * LANES)
        for piece, part in enumerate(parts)
        for b in range(part.shape[1] // LANES)
    ]

    def write(side):
        copies = []
        for n in range(half // LANES):
            piece, base = places[side * (half // LANES) + n]
            at = slice(base, base + LANES)
            here = slice(n * LANES, (n + 1) * LANES)
            to = slice(side * half + n * LANES, side * half + (n + 1) * LANES)
            start = carry[:, here].astype(F32)
            middle = jnp.exp(-rates_pc[:, to] * SUB) * start + state[:, here]
            before = jnp.concatenate(
                [spread_groups(start, per_group, poles), spread_groups(middle, per_group, poles)],
                axis=1,
            )
            lifted = dot(lifts[piece][:, at], before)
            for k in range(2):
                rows = slice(k * SUB, (k + 1) * SUB)
                long_out = parts[piece][rows, at] + lifted[:, k * LANES : (k + 1) * LANES]
                out[rows, here] = (gates[piece][rows, at].astype(F32) * long_out).astype(BF16)
            if (n + 1) * LANES % CHUNK == 0:
                first = (n + 1) * LANES - CHUNK
                copy = pltpu.make_async_copy(
                    out.at[:, pl.ds(first, CHUNK)],
                    mixed.at[:, pl.ds(side * half + first, CHUNK)],
                    sems.at[first // CHUNK],
                )
                copy.start()
                copies.append(copy)
        for copy in copies:
            copy.wait()

    for core in range(2):
        pl.when(upper == core)(functools.partial(write, core if followed else 1 - core))


HBM, VMEM, FREE = "hbm", "vmem", "free"


def call(kernel, in_specs, outs, scratch, name, flops, args, aliases={}):
    moved = sum(a.size * a.dtype.itemsize for a in args)
    moved += sum(s.size * s.dtype.itemsize for s, _ in outs)
    spaces = {HBM: pltpu.HBM, VMEM: pltpu.VMEM}
    where = {key: pl.BlockSpec(memory_space=spaces.get(key, pltpu.VMEM)) for key in (HBM, VMEM, FREE)}
    args = [
        pltpu.with_memory_space_constraint(a, spaces[spec]) if spec in spaces else a
        for a, spec in zip(args, in_specs)
    ]
    return pl.pallas_call(
        kernel,
        in_specs=[where[spec] for spec in in_specs],
        out_specs=[where[spec] for _, spec in outs],
        out_shape=[
            pltpu.VMEM(shape.shape, shape.dtype) if spec is VMEM else shape for shape, spec in outs
        ],
        scratch_shapes=scratch,
        input_output_aliases=aliases,
        compiler_params=pltpu.CompilerParams(vmem_limit_bytes=20 << 20),
        cost_estimate=pl.CostEstimate(flops=flops, bytes_accessed=moved, transcendentals=0),
        name=name,
    )(*args)


def swap(value, distance):
    count = lax.axis_size("seq")
    route = [(i, i ^ distance) for i in range(count) if i ^ distance < count]
    return lax.ppermute(value, "seq", route)


def chip_kernel(positions, total, partner, rates_pc, chip, before, message, rates):
    half = chip.shape[1]
    upper = lax.axis_index("seq") % 2
    above = upper == 1
    mine, theirs = total[...], partner[...].astype(F32)
    rate = rates_pc[:, pl.ds(pl.multiple_of(upper * half, LANES), half)]
    whole = jnp.exp(-rate * positions) * jnp.where(above, theirs, mine)
    whole += jnp.where(above, mine, theirs)
    chip[...] = whole
    before[...] = jnp.zeros_like(whole)
    message[...] = whole.astype(BF16)
    rates[...] = rate


def grown(positions, size, chip, received, before, rates):
    index = lax.axis_index("seq")
    above = (index // size) % 2 == 1
    behind = ((index % size) // 2 * 2 * positions).astype(F32)
    rate, mine, theirs = rates[...], chip[...], received[...].astype(F32)
    earlier = before[...] + jnp.where(above, jnp.exp(-rate * behind) * theirs, 0.0)
    whole = jnp.exp(-rate * (positions * size)) * jnp.where(above, theirs, mine)
    return earlier, whole + jnp.where(above, mine, theirs)


def round_kernel(
    positions, size, chip, received, before, rates, _, chip_out, before_out, message
):
    before_out[...], whole = grown(positions, size, chip, received, before, rates)
    chip_out[...] = whole
    message[...] = whole.astype(BF16)


def last_kernel(
    positions, size, chip, received, before, rates, total, partner, _, carry, message
):
    upper = lax.axis_index("seq") % 2 == 1
    earlier, _ = grown(positions, size, chip, received, before, rates)
    lower = jnp.where(upper, partner[...].astype(F32), total[...])
    after = jnp.exp(-rates[...] * positions) * earlier + lower
    carry[...] = jnp.where(upper, after, earlier)
    message[...] = jnp.where(upper, earlier, after).astype(BF16)


def scan_states(total, partner, rates_pc, positions, fill):
    count = lax.axis_size("seq")
    half = jax.ShapeDtypeStruct(total.shape, F32)
    packed = jax.ShapeDtypeStruct(total.shape, BF16)
    chip, before, message, rates = call(
        functools.partial(chip_kernel, positions), [VMEM] * 3,
        [(half, VMEM), (half, VMEM), (packed, VMEM), (half, VMEM)],
        [], "chip", total.size, (total, partner, rates_pc),
    )
    size = 2
    while True:
        message, filled = fill(message)
        received = swap(message, size)
        held = (chip, received, before, rates)
        if 2 * size >= count:
            break
        chip, before, message = call(
            functools.partial(round_kernel, positions, size), [VMEM] * 5,
            [(half, VMEM), (half, VMEM), (packed, VMEM)],
            [], "round", total.size, (*held, filled),
        )
        size *= 2
    carry, message = call(
        functools.partial(last_kernel, positions, size), [VMEM] * 7,
        [(half, VMEM), (packed, VMEM)],
        [], "last", total.size, (*held, total, partner, filled),
    )
    message, _ = fill(message)
    return carry, swap(message, 1)


def shards(
    gate_out, gate_in, values, gate_mid, medium_taps, medium_skip, residues, rates, long_skip
):
    row_count, features = gate_out.shape
    groups, poles = rates.shape
    per_group = features // groups
    count = lax.axis_size("seq")
    cuts = [features // LANES * k // 32 * LANES for k in (0, 12, 22, 32)]
    shape = jax.ShapeDtypeStruct
    dma = pltpu.SemaphoreType.DMA
    chunks = features // CHUNK

    (tail,) = call(
        tail_kernel,
        [HBM, HBM],
        [(shape((SUB, features), BF16), VMEM)],
        [pltpu.VMEM((2, SUB, features), BF16), dma((chunks, 2))],
        "tail",
        SUB * features,
        (gate_in, values),
    )
    halo = lax.ppermute(tail, "seq", [(i, i + 1) for i in range(count - 1)])

    rate_rows = rates.reshape(-1, LANES)
    residue_rows = residues.reshape(-1, LANES)
    med_skip = medium_skip[None]
    lng_skip = long_skip[None]
    rate_rows, residue_rows, med_skip, lng_skip = lax.optimization_barrier(
        (rate_rows, residue_rows, med_skip, lng_skip)
    )
    per_pole = shape((poles, features), F32)
    half_rows = shape((SUB, features), BF16)

    med_strips, folds, rates_pc, product, mid_first, gated_b, later = call(
        functools.partial(early_kernel, per_group, poles),
        [HBM, HBM, HBM, FREE, FREE, FREE],
        [
            (shape((groups * STRIP, MED + STRIP), BF16), VMEM),
            (shape((groups * poles, SUB), BF16), VMEM),
            (per_pole, VMEM),
            (half_rows, VMEM),
            (half_rows, VMEM),
            (half_rows, VMEM),
            (per_pole, VMEM),
        ],
        [
            pltpu.VMEM((row_count, features), BF16),
            pltpu.VMEM((row_count, features), BF16),
            pltpu.VMEM((SUB, features), BF16),
            pltpu.VMEM((groups, 2 * LANES), F32),
            dma((chunks, 4)),
        ],
        "early",
        2 * SUB * SUB * features * 8,
        (gate_in, values, gate_mid, medium_taps, rate_rows, med_skip),
    )
    half_states = shape((poles, features // 2), F32)

    def late(followed, med_skip):
        return call(
            functools.partial(late_kernel, per_group, poles, followed),
            [VMEM] * 6 + [FREE, VMEM],
            [
                (shape((SUB, features // 2), BF16), VMEM),
                (half_states, VMEM),
                (half_states, VMEM),
                (shape((poles, features // 2), BF16), VMEM),
            ],
            [],
            "late",
            SUB * SUB * features * 8,
            (halo, product, mid_first, med_strips, folds, rates_pc, med_skip, later),
        )

    other_a, other_state, _, message = late(False, med_skip)
    message, held = lax.optimization_barrier((message, med_skip))
    partner = swap(message, 1)
    own_a, own_state, total, _ = late(True, held)

    def inner(piece, residue_rows):
        width = cuts[piece + 1] - cuts[piece]
        return call(
            functools.partial(inner_kernel, per_group, poles, cuts[piece]),
            [VMEM, VMEM, VMEM, FREE, FREE, FREE, HBM],
            [
                (shape((row_count, width), F32), VMEM),
                (shape((SUB, width), BF16), VMEM),
                (shape((row_count, width), BF16), VMEM),
                (shape((1, LANES), F32), VMEM),
            ],
            [
                pltpu.VMEM((width // per_group, LANES), BF16),
                pltpu.VMEM((width // per_group, 2 * LANES), F32),
                pltpu.VMEM((SUB, width), BF16),
                dma,
            ],
            f"inner{piece}",
            4 * SUB * SUB * width * 8,
            (other_a, own_a, gated_b, rate_rows, residue_rows, lng_skip, gate_out),
        )

    pieces = []

    def fill(message):
        if len(pieces) < PIECES:
            message, held = lax.optimization_barrier((message, residue_rows))
            pieces.append(inner(len(pieces), held))
        return message, pieces[-1][-1]

    carry, other = scan_states(total, partner, rates_pc, row_count, fill)
    while len(pieces) < PIECES:
        fill(other)
    parts, lifts, gates, _ = zip(*pieces)

    def final(followed, carry, state, *earlier):
        (mixed,) = call(
            functools.partial(final_kernel, per_group, poles, followed),
            [VMEM] * (3 + 3 * PIECES) + [HBM] * len(earlier),
            [(shape((row_count, features), BF16), HBM)],
            [pltpu.VMEM((row_count, features // 2), BF16), dma((chunks // 2,))],
            "final",
            SUB * SUB * features * 2,
            (carry, state, rates_pc, *parts, *lifts, *gates, *earlier),
            {3 + 3 * PIECES: 0} if earlier else {},
        )
        return mixed

    mixed = final(True, carry, own_state)
    return final(False, other, other_state, mixed)


def solution(mesh):
    rows = P(("grp", "seq"), None)
    return jax.shard_map(
        shards,
        mesh=mesh,
        in_specs=(rows,) * 4 + (P(),) * 5,
        out_specs=rows,
        check_vma=False,
    )
```
